512 devices in a mesh: tile: 32 (over y, x, core), fsdp: 16 (over z).
Axes of the slice: x: 4, y: 4, z: 16, core: 2. Of those that a mesh axis runs over, the one named last changes fastest.
Arguments:
- images: bfloat16 [16, 32, 8, 128, 320], P('fsdp', 'tile'), may hold values from -80 to 80
- tile_rows: int32 [16, 32], P('fsdp', 'tile'), may hold values from 1 to 8, 160 in all within a row
- cotangent: bfloat16 [16, 32, 8, 128, 320], P('fsdp', 'tile'), may hold values from -6 to 6
- master_weight: float32 [2880, 320], P('fsdp'), may hold values from -0.109375 to 0.109375
- norm_gain: float32 [320], replicated, may hold values from 0.5 to 1.5
- norm_bias: float32 [320], replicated, may hold values from -3 to 3
- first_moment: float32 [2880, 320], P('fsdp'), may hold values from -6 to 6
- second_moment: float32 [2880, 320], P('fsdp'), may hold values from 0.5 to 4
Outputs:
- activation: bfloat16 [16, 32, 8, 128, 320], P('fsdp', 'tile')
- image_grad: bfloat16 [16, 32, 8, 128, 320], P('fsdp', 'tile')
- weight_grad: float32 [2880, 320], P('fsdp')
- new_weight: float32 [2880, 320], P('fsdp')
- new_first: float32 [2880, 320], P('fsdp')
- new_second: float32 [2880, 320], P('fsdp')
- gain_grad: float32 [320], replicated
- bias_grad: float32 [320], replicated
The draws below stay inside these ranges and needn't reach their ends.
Inputs may be any that keep to these rules, and one draw needn't show every extreme that they name: `tile_rows`: in each frame the 32 counts sum to 160 and the largest is exactly 8.
All inputs are finite; a program needn't handle non-finite values. No bound on the sum of `tile_rows` on one device may be relied on, other than what follows from the above.
Results may differ from the reference program's by a relative error of at most 0.027.
Values may be sent and summed in bfloat16 or wider, within the bound.
No kernel may reach another device: no remote copies, remote signals or barrier semaphores. Data moves between devices by JAX's collectives and lax.ppermute only.
A program may use at most 64 MiB of HBM per device.

```python
import math
import jax
import jax.numpy as jnp
import numpy as np
from jax import lax

C = 320
GROUPS = 32
COLS = 128
CAP = 8
FRAMES = 16
FRAME_ROWS = 160
CELLS = 327680
N_TILE = 32


def draw_images(key, part):
    k_base, k_chan, k_row, k_mean = jax.random.split(key, 4)
    shape = (FRAMES, N_TILE, CAP, COLS, C)
    common = 0.5 * jnp.clip(jax.random.normal(k_mean, (FRAMES, 1, 1, 1, C), jnp.float32), -2.0, 2.0)
    base = jnp.clip(jax.random.normal(k_base, shape, jnp.float32), -3.0, 3.0) + common
    position = jnp.arange(N_TILE, dtype=jnp.float32) / max(N_TILE - 1, 1)
    along = jnp.exp(position * math.log(3.0)).reshape(1, N_TILE, 1, 1, 1)
    channel_scale = jnp.exp(jax.random.uniform(k_chan, (FRAMES, 1, 1, 1, C), jnp.float32) * math.log(10.0)) / 3.0
    row_scale = jnp.exp(jax.random.uniform(k_row, (FRAMES, N_TILE, CAP, 1, 1), jnp.float32) * math.log(2.0))
    return (base * along * channel_scale * row_scale).astype(jnp.bfloat16)


def block_levels(own_key, shape, cuts, least, high):
    gain, own = 1.0, jax.random.fold_in(own_key, 6)
    for dim, shards_of in cuts:
        draws = jnp.exp(jax.random.uniform(jax.random.fold_in(own, dim), (shards_of,), jnp.float32, least / len(cuts), high / len(cuts)))
        gain = gain * jnp.repeat(draws, shape[dim] // shards_of).reshape([-1 if axis == dim else 1 for axis in range(len(shape))])
    return gain


def length_profile(amount, total, reach, skew):
    loads = [(1 << 20) // math.isqrt(standing ** skew) + 1 for standing in range(2, amount + 1)]
    surplus, given = total - reach - (amount - 1), [1] * (amount - 1)
    while surplus > 0:
        free = [i for i in range(amount - 1) if given[i] < reach]
        whole, budget = sum([loads[i] for i in free]), surplus
        for i in free:
            addition = min(reach - given[i], max(1, budget * loads[i] // whole), surplus)
            given[i] = given[i] + addition
            surplus = surplus - addition
    return np.array([reach] + given)


def uneven_parts(key, amount, total, most, lean):
    if amount == 2:
        one = jax.random.randint(key, (), max(1, total - most), min(most, total - 1) + 1)
        return jnp.stack([one, total - one])
    tallies = jnp.asarray(length_profile(amount, total, most, lean), jnp.int32)
    couples = (amount - 1) // 2
    giver, sink = tallies[1:1 + 2 * couples:2], tallies[2:2 + 2 * couples:2]
    slack = jnp.minimum(giver - 1, most - sink)
    passed = jax.random.randint(jax.random.fold_in(key, 1), (couples,), 0, 1 << 20) % (slack + 1)
    tallies = tallies.at[1:1 + 2 * couples:2].set(giver - passed).at[2:2 + 2 * couples:2].set(sink + passed)
    return tallies[jax.random.permutation(jax.random.fold_in(key, 2), amount)]


def bell_draw(own_key, dims, deviation, reach, cuts=(), kind=jnp.bfloat16):
    gain = block_levels(own_key, dims, cuts, -0.22, 0.18) if cuts else 1.0
    array = jax.random.normal(own_key, dims, jnp.float32) * deviation * gain
    return jnp.minimum(jnp.maximum(array, -reach), reach).astype(kind)


def setup_inputs(seed: int = 0) -> dict:
    keys = jax.random.split(jax.random.key(seed), 9)
    return {
        "images": draw_images(jax.random.fold_in(keys[8], 71), 0),
        "tile_rows": jax.vmap(lambda own: uneven_parts(own, N_TILE, FRAME_ROWS, CAP, 2))(jax.random.split(keys[1], FRAMES)).reshape((FRAMES, N_TILE)).astype(jnp.int32),
        "cotangent": bell_draw(keys[2], (FRAMES, N_TILE, CAP, COLS, C), 1.0, 6.0, ((0, 16), (1, 32))),
        "master_weight": bell_draw(keys[3], (9 * C, C), (9 * C) ** -0.5, 0.109375, ((0, 16),), jnp.float32),
        "norm_gain": jnp.clip(1.0 + 0.1 * jax.random.normal(keys[4], (C,), jnp.float32), 0.5, 1.5),
        "norm_bias": bell_draw(keys[5], (C,), 0.5, 3.0, (), jnp.float32),
        "first_moment": bell_draw(keys[6], (9 * C, C), 1.0, 6.0, ((0, 16),), jnp.float32),
        "second_moment": jnp.clip(jnp.exp(math.log(4.0) - 2.0794415 * jax.random.uniform(keys[7], (9 * C, C), jnp.float32) ** block_levels(keys[7], (9 * C, C), ((0, 16),), -0.2, 0.2)), 0.5, 4.0),
    }


def shifted_taps(picture):
    height, breadth = (picture.shape[0], picture.shape[1])
    padded = jnp.pad(picture, ((1, 1), (1, 1), (0, 0)))
    return [padded[row_step:row_step + height, col_step:col_step + breadth, :] for row_step in range(3) for col_step in range(3)]

def convolve(picture, kernel):
    channels = picture.shape[2]
    output = jnp.zeros((picture.shape[0] * picture.shape[1], kernel.shape[1]), jnp.float32)
    for tap_index, piece in enumerate(shifted_taps(picture)):
        output = output + jnp.dot(piece.reshape(-1, channels), kernel[tap_index * channels:(tap_index + 1) * channels], preferred_element_type=jnp.float32)
    return output

def reference(images, tile_rows, cotangent, master_weight, norm_gain, norm_bias, first_moment, second_moment):
    per_group = C // GROUPS
    kernel = master_weight.astype(jnp.bfloat16)
    flipped = kernel.reshape(9, C, C)[::-1].transpose(0, 2, 1).reshape(9 * C, C)
    population = jnp.float32(FRAME_ROWS * COLS * per_group)

    def grouped(values):
        return lax.optimization_barrier(jnp.sum(values.reshape(-1, GROUPS, per_group), axis=(0, 2)))

    def spread(stat):
        return jnp.repeat(stat, per_group)

    def one_frame(carry, inputs):
        kernel_sum, gain_sum, bias_sum = carry
        pictures, counts, upstream_in = inputs
        offsets = (jnp.cumsum(counts) - counts).astype(jnp.int32)
        slot_index = jnp.arange(CAP, dtype=jnp.int32)
        live = slot_index[None, :] < counts[:, None]
        target = jnp.where(live, offsets[:, None] + slot_index[None, :], FRAME_ROWS).reshape(-1).astype(jnp.int32)

        def compact(slot_data):
            holder = jnp.zeros((FRAME_ROWS + 1, COLS, C), slot_data.dtype)
            return holder.at[target].set(slot_data.reshape(-1, COLS, C))[:FRAME_ROWS]

        def expand(frame_data):
            extended = jnp.concatenate([frame_data, jnp.zeros((1, COLS, C), frame_data.dtype)], axis=0)
            return extended[target].reshape(N_TILE, CAP, COLS, C)
        picture = compact(pictures)
        mixed = convolve(picture, kernel)
        group_mean = grouped(mixed) / population
        centered = mixed - spread(group_mean)
        variance = grouped(centered * centered) / population
        inverse = lax.rsqrt(variance + 1e-05)
        normed = centered * spread(inverse)
        shifted = normed * norm_gain + norm_bias
        gate_value = jax.nn.sigmoid(shifted)
        activation = (shifted * gate_value).astype(jnp.bfloat16)
        upstream = compact(upstream_in).reshape(-1, C).astype(jnp.float32)
        dshift = upstream * gate_value * (1.0 + shifted * (1.0 - gate_value))
        scaled = dshift * norm_gain
        delta_mean = grouped(scaled) / population
        cross_mean = grouped(scaled * normed) / population
        pre_grad = (spread(inverse) * (scaled - spread(delta_mean) - normed * spread(cross_mean))).astype(jnp.bfloat16)
        grad_picture = pre_grad.reshape(FRAME_ROWS, COLS, C)
        image_grad = convolve(grad_picture, flipped).astype(jnp.bfloat16)
        blocks = [jnp.dot(piece.reshape(-1, C).T, pre_grad, preferred_element_type=jnp.float32) for piece in shifted_taps(picture)]
        kernel_sum = kernel_sum + jnp.concatenate(blocks, axis=0)
        gain_sum = gain_sum + lax.optimization_barrier(jnp.sum(dshift * normed, axis=0))
        bias_sum = bias_sum + lax.optimization_barrier(jnp.sum(dshift, axis=0))
        outputs = (expand(activation.reshape(FRAME_ROWS, COLS, C)), expand(image_grad.reshape(FRAME_ROWS, COLS, C)))
        return ((kernel_sum, gain_sum, bias_sum), outputs)
    start_carry = (jnp.zeros((9 * C, C), jnp.float32), jnp.zeros((C,), jnp.float32), jnp.zeros((C,), jnp.float32))
    totals, stacked = lax.scan(one_frame, start_carry, (images, tile_rows, cotangent))
    norm_scale = jnp.float32(CELLS) ** (-0.5)
    weight_grad = totals[0] * norm_scale
    new_first = 0.9 * first_moment + 0.1 * weight_grad
    new_second = 0.999 * second_moment + 0.001 * weight_grad * weight_grad
    first_fix = new_first / (1.0 - 0.9 ** 10)
    second_fix = new_second / (1.0 - 0.999 ** 10)
    new_weight = master_weight - 0.01 * first_fix / (jnp.sqrt(second_fix) + 1e-08)
    return (stacked[0], stacked[1], weight_grad, new_weight, new_first, new_second, totals[1] * norm_scale, totals[2] * norm_scale)
```

```python
import jax
import jax.numpy as jnp
from jax import lax
from jax.sharding import Mesh, PartitionSpec as P

GROUPS = 32
ROWS_MEAN = 5
PIECE = 24
TILE = ("y", "x", "core")


def beside(first_row, last_row):
    count = 32
    ends = count - 1
    above = lax.ppermute(last_row, TILE, [(i, (i + 1) % count) for i in range(ends)])
    below = lax.ppermute(first_row, TILE, [((i + 1) % count, i) for i in range(ends)])
    return above, below


def framed(source, above, below, live_count):
    slot_count = source.shape[0]
    zero_row = jnp.zeros_like(source[0:1])
    stacked = jnp.concatenate([above, source, zero_row], axis=0)
    marker = (jnp.arange(slot_count + 2) == live_count + 1)[:, None, None]
    stacked = jnp.where(marker, below, stacked)
    return jnp.pad(stacked, ((0, 0), (1, 1), (0, 0)))


def patches_of(padded, slot_count, cell_cols):
    pieces = [
        padded[row_step : row_step + slot_count, col_step : col_step + cell_cols, :]
        for row_step in range(3)
        for col_step in range(3)
    ]
    return jnp.concatenate(pieces, axis=-1).reshape(slot_count * cell_cols, -1)


def gather_equal(value, axes, count):
    copies = jnp.broadcast_to(value, (count,) + value.shape)
    return lax.all_to_all(copies, axes, 0, 0)


def other_core(value):
    return lax.ppermute(value, "core", [(0, 1), (1, 0)])


def gather_weights(shard):
    core, y = lax.axis_index("core"), lax.axis_index("y")
    channels = shard.shape[1]
    rows = shard.shape[0]
    padded = jnp.pad(shard.astype(jnp.bfloat16), ((0, 8 * PIECE - rows), (0, 0)))
    pieces = padded.reshape(8, PIECE, channels)
    mine = lax.dynamic_index_in_dim(pieces, core * 4 + y, 0, keepdims=False)
    along_z = gather_equal(mine, "fsdp", 16)
    along_y = gather_equal(along_z, "y", 4)
    passed = other_core(along_y)
    first = core == 0
    both = jnp.stack([jnp.where(first, along_y, passed), jnp.where(first, passed, along_y)])
    ordered = both.transpose(2, 0, 1, 3, 4).reshape(16, 8 * PIECE, channels)
    return ordered[:, :rows].reshape(16 * rows, channels)


def reduce_weights(partial, gain_total, bias_total, rows):
    core, y = lax.axis_index("core"), lax.axis_index("y")
    channels = partial.shape[1]
    blocks = jnp.pad(partial.reshape(16, rows, channels), ((0, 0), (0, 8 * PIECE - rows), (0, 0)))
    blocks = blocks.reshape(16, 2, 4, PIECE, channels).transpose(1, 2, 0, 3, 4)
    blocks = blocks.astype(jnp.bfloat16)
    keep = lax.dynamic_index_in_dim(blocks, core, 0, keepdims=False)
    send = lax.dynamic_index_in_dim(blocks, 1 - core, 0, keepdims=False)
    pair = (keep.astype(jnp.float32) + other_core(send).astype(jnp.float32)).astype(jnp.bfloat16)
    quads = lax.all_to_all(pair, "y", 0, 0)
    quad = jnp.sum(quads.astype(jnp.float32), axis=0)
    extra = jnp.stack([gain_total, bias_total])
    high = extra.astype(jnp.bfloat16).astype(jnp.float32)
    rider = jnp.concatenate([high, extra - high], axis=0)
    slot = rows - 7 * PIECE
    rider = jnp.pad(rider, ((slot, PIECE - slot - 4), (0, 0)))
    last = (core * 4 + y) == 7
    quad = (quad + jnp.where(last, rider, 0.0)[None]).astype(jnp.bfloat16)
    frames = lax.all_to_all(quad, "fsdp", 0, 0)
    frame_sum = jnp.sum(frames.astype(jnp.float32), axis=0)
    tiles = gather_equal(frame_sum, TILE, 32).reshape(4, 4, 2, PIECE, channels)
    shard = jnp.sum(tiles, axis=1).transpose(1, 0, 2, 3).reshape(8 * PIECE, channels)
    riders = tiles[3, 0, 1, slot : slot + 4]
    return shard[:rows], riders[0] + riders[2], riders[1] + riders[3]


def local(
    images, tile_rows, cotangent, master_weight, norm_gain, norm_bias, first_moment, second_moment
):
    slot_count, cell_cols, channels = (images.shape[2], images.shape[3], images.shape[4])
    per_group = channels // GROUPS
    population = jnp.float32(ROWS_MEAN * 32 * cell_cols * per_group)
    live_count = tile_rows[0, 0]
    live_rows = jnp.arange(slot_count) < live_count
    cell_mask = jnp.repeat(live_rows, cell_cols).astype(jnp.float32)[:, None]

    def grouped(values):
        return jnp.sum(values.reshape(-1, GROUPS, per_group), axis=(0, 2))

    def spread(stat):
        return jnp.repeat(stat, per_group)

    source = jnp.where(live_rows[:, None, None], images[0, 0], jnp.zeros((), jnp.bfloat16))
    above, below = beside(
        source[0:1], lax.dynamic_slice_in_dim(source, live_count - 1, 1, 0)
    )
    columns = patches_of(framed(source, above, below, live_count), slot_count, cell_cols)
    gathered = gather_weights(master_weight)
    mixed = jnp.dot(columns, gathered, preferred_element_type=jnp.float32)
    own_count = live_count.astype(jnp.float32) * (cell_cols * per_group)
    own_sum = grouped(mixed * cell_mask)
    own_centered = (mixed - spread(own_sum / own_count)) * cell_mask
    own_square = grouped(own_centered * own_centered)
    message = jnp.concatenate([own_sum, own_square, jnp.full((64,), own_count)])
    stats = gather_equal(message, TILE, 32)
    sums, squares, counts = stats[:, :32], stats[:, 32:64], stats[:, 64:65]
    group_mean = jnp.sum(sums, axis=0) / population
    offset = sums / counts - group_mean
    variance = jnp.sum(squares + counts * offset * offset, axis=0) / population
    inverse = lax.rsqrt(variance + 1e-05)
    normed = (mixed - spread(group_mean)) * spread(inverse)
    shifted = normed * norm_gain + norm_bias
    gate_value = jax.nn.sigmoid(shifted)
    activation = (shifted * gate_value * cell_mask).astype(jnp.bfloat16).reshape(images.shape)
    upstream = cotangent[0, 0].reshape(-1, channels).astype(jnp.float32) * cell_mask
    dshift = upstream * gate_value * (1.0 + shifted * (1.0 - gate_value))
    scaled = dshift * norm_gain
    per_channel = jnp.concatenate([jnp.sum(dshift * normed, axis=0), jnp.sum(dshift, axis=0)])
    totals = jnp.sum(gather_equal(per_channel, TILE, 32), axis=0)
    gain_total, bias_total = totals[:channels], totals[channels:]
    delta_sum = jnp.sum((bias_total * norm_gain).reshape(GROUPS, per_group), axis=1)
    cross_sum = jnp.sum((gain_total * norm_gain).reshape(GROUPS, per_group), axis=1)
    norm_scale = jnp.float32(16 * ROWS_MEAN * 32 * cell_cols) ** (-0.5)
    pre_grad = spread(inverse) * (
        scaled - spread(delta_sum / population) - normed * spread(cross_sum / population)
    )
    pre_grad = (pre_grad * cell_mask).astype(jnp.bfloat16)
    grad_field = pre_grad.reshape(slot_count, cell_cols, channels)
    above_grad, below_grad = beside(
        grad_field[0:1], lax.dynamic_slice_in_dim(grad_field, live_count - 1, 1, 0)
    )
    partial = lax.dot_general(
        columns, pre_grad, (((0,), (0,)), ((), ())), preferred_element_type=jnp.float32
    )
    rows = master_weight.shape[0]
    grad_shard, gain_all, bias_all = reduce_weights(partial, gain_total, bias_total, rows)
    grad_columns = patches_of(
        framed(grad_field, above_grad, below_grad, live_count), slot_count, cell_cols
    )
    flipped = (
        gathered.reshape(9, channels, channels)[::-1]
        .transpose(0, 2, 1)
        .reshape(9 * channels, channels)
    )
    image_grad = (
        (jnp.dot(grad_columns, flipped, preferred_element_type=jnp.float32) * cell_mask)
        .astype(jnp.bfloat16)
        .reshape(images.shape)
    )
    weight_grad = grad_shard * norm_scale
    new_first = 0.9 * first_moment + 0.1 * weight_grad
    new_second = 0.999 * second_moment + 0.001 * weight_grad * weight_grad
    first_fix = new_first / (1.0 - 0.9**10)
    second_fix = new_second / (1.0 - 0.999**10)
    new_weight = master_weight - 0.01 * first_fix / (jnp.sqrt(second_fix) + 1e-08)
    return (
        activation,
        image_grad,
        weight_grad,
        new_weight,
        new_first,
        new_second,
        gain_all * norm_scale,
        bias_all * norm_scale,
    )


def solution(mesh):
    fine = Mesh(mesh.devices.reshape(4, 4, 2, 16), ("y", "x", "core", "fsdp"))
    pixels = P("fsdp", TILE, None, None, None)
    placed = (
        pixels,
        P("fsdp", TILE),
        pixels,
        P("fsdp", None),
        P(),
        P(),
        P("fsdp", None),
        P("fsdp", None),
    )
    return jax.shard_map(
        local,
        mesh=fine,
        in_specs=placed,
        out_specs=(
            pixels,
            pixels,
            P("fsdp", None),
            P("fsdp", None),
            P("fsdp", None),
            P("fsdp", None),
            P(),
            P(),
        ),
        check_vma=False,
    )
```

```python
import functools
import jax
import jax.numpy as jnp
from jax import lax
from jax.experimental import pallas as pl
from jax.experimental.pallas import tpu as pltpu
from jax.sharding import Mesh, PartitionSpec as P

TILE = ("y", "x", "core")
CH = 320
PER = 10
COLS = 128
CAP = 8
SHARD = 180
WIDE = 192
DEEP = 16 * WIDE
ROWS = 40
LANES = 256
POPULATION = 204800.0
SCALE = 327680.0 ** -0.5
BF = jnp.bfloat16
F32 = jnp.float32
VMEM = pl.BlockSpec(memory_space=pltpu.VMEM)
SMEM = pl.BlockSpec(memory_space=pltpu.SMEM)


def spot(name):
    return lax.axis_index(name)


def call(body, outs, ins, scratch=(), grid=None, cost=1, room=16, **more):
    if grid is not None:
        more["grid"] = grid
    return pl.pallas_call(
        body,
        out_shape=outs,
        in_specs=ins,
        scratch_shapes=list(scratch),
        compiler_params=pltpu.CompilerParams(vmem_limit_bytes=room << 20),
        cost_estimate=pl.CostEstimate(
            flops=cost * 1000000000, bytes_accessed=cost << 21, transcendentals=0
        ),
        **more,
    )


def shape(dims, kind=F32):
    return jax.ShapeDtypeStruct(dims, kind)


def pack_body(weight, out, padded, turned):
    padded[...] = jnp.zeros(padded.shape, F32)
    padded[0:SHARD, 0:CH] = weight[...]
    turned[...] = jnp.transpose(padded[...])
    piece = spot("core") * 4 + spot("y")
    rows = turned[pl.ds(pl.multiple_of(piece * ROWS, 8), ROWS), :]
    odd = (spot("fsdp") % 2) == 1
    rows = jnp.where(odd, pltpu.roll(rows, 64, 1), rows).astype(BF)
    for frame in range(16):
        out[frame] = rows


def pack(weight):
    return call(
        pack_body,
        shape((16, ROWS, LANES), BF),
        [VMEM],
        [pltpu.VMEM((256, 384), F32), pltpu.VMEM((384, 256), F32)],
        out_specs=VMEM,
    )(weight)


def store_taps(row, field, slot, negate):
    lane = lax.broadcasted_iota(jnp.int32, (CH, COLS), 1)
    for b in range(3):
        turn = (1 - b) if not negate else (b - 1)
        if turn == 0:
            moved = row
        elif turn == 1:
            moved = jnp.where(lane == 0, 0.0, pltpu.roll(row, 1, 1))
        else:
            moved = jnp.where(lane == COLS - 1, 0.0, pltpu.roll(row, COLS - 1, 1))
        for a in range(3):
            up = a if not negate else 2 - a
            r = slot - up
            if 0 <= r < CAP:
                field(3 * a + b, r, moved)


def framed_row(slot, own, above, below, live):
    if slot == 0:
        return above[0].astype(F32)
    base = own[slot - 1].astype(F32) if slot <= CAP else jnp.zeros((CH, COLS), F32)
    if slot == 1:
        return base
    under = below[0].astype(F32)
    return jnp.where(slot - 1 < live, base, jnp.where(slot - 1 == live, under, 0.0))


def patch_body(live_ref, own, above, below, out, wide):
    live = live_ref[0, 0]

    def put(tap, r, value):
        start = tap * CH
        while start < (tap + 1) * CH:
            frame = start // SHARD
            stop = min((frame + 1) * SHARD, (tap + 1) * CH)
            wide[r, start + 12 * frame : stop + 12 * frame, :] = value[
                start - tap * CH : stop - tap * CH
            ]
            start = stop

    for frame in range(16):
        first = frame * WIDE + SHARD
        wide[:, first : first + 12, :] = jnp.zeros((CAP, 12, COLS), F32)
    for slot in range(CAP + 2):
        store_taps(framed_row(slot, own, above, below, live), put, slot, False)
    for r in range(CAP):
        out[:, r * COLS : (r + 1) * COLS] = wide[r].astype(BF)


def patches(live, own, above, below):
    return call(
        patch_body,
        shape((DEEP, CAP * COLS), BF),
        [SMEM, VMEM, VMEM, VMEM],
        [pltpu.VMEM((CAP, DEEP, COLS), F32)],
        out_specs=VMEM,
        cost=8,
        room=30,
    )(live, own, above, below)


def one_hot():
    channel = lax.broadcasted_iota(jnp.int32, (CH, COLS), 0)
    lane = lax.broadcasted_iota(jnp.int32, (CH, COLS), 1) * PER
    return jnp.where((channel >= lane) & (channel < lane + PER), 1.0, 0.0)


def to_groups(column, hot):
    return jnp.sum(column * hot, axis=0, keepdims=True)


def from_groups(row, hot):
    return jnp.broadcast_to(jnp.sum(row * hot, axis=1, keepdims=True), (CH, COLS))


def forward_body(live_ref, mine, other, patch, mixed, weight, message):
    step = pl.program_id(0)

    @pl.when(step == 0)
    def _():
        left = lax.broadcasted_iota(jnp.int32, (ROWS, COLS), 1) < 64
        for half, source in ((0, mine), (1, other)):
            side = (spot("core") + half) % 2
            for y in range(4):
                base = pl.multiple_of(side * 160 + y * ROWS, 8)
                for pair in range(8):
                    even, odd = source[y, 2 * pair], source[y, 2 * pair + 1]
                    middle = jnp.where(left, even[:, 128:].astype(F32), odd[:, :128].astype(F32))
                    at = pair * 384
                    weight[pl.ds(base, ROWS), at : at + 128] = even[:, :128]
                    weight[pl.ds(base, ROWS), at + 128 : at + 256] = middle.astype(BF)
                    weight[pl.ds(base, ROWS), at + 256 : at + 384] = odd[:, 128:]

    block = jnp.dot(weight[...], patch[...], preferred_element_type=F32)
    mixed[2 * step] = block[:, :128]
    mixed[2 * step + 1] = block[:, 128:]

    @pl.when(step == 3)
    def _():
        live = live_ref[0, 0]
        hot = one_hot()
        total = jnp.zeros((CH, COLS), F32)
        for r in range(CAP):
            total = total + jnp.where(r < live, mixed[r], 0.0)
        column = jnp.broadcast_to(jnp.sum(total, axis=1, keepdims=True), (CH, COLS))
        sums = to_groups(column, hot)
        count = live.astype(F32) * (COLS * PER)
        mean = from_groups(sums / count, hot)
        square = jnp.zeros((CH, COLS), F32)
        for r in range(CAP):
            away = mixed[r] - mean
            square = square + jnp.where(r < live, away * away, 0.0)
        column = jnp.broadcast_to(jnp.sum(square, axis=1, keepdims=True), (CH, COLS))
        squares = to_groups(column, hot)
        line = lax.broadcasted_iota(jnp.int32, (8, COLS), 0)
        note = jnp.where(line == 0, sums, jnp.where(line == 1, squares, count))
        for tile in range(32):
            message[tile] = note


def forward(live, mine, other, patch):
    whole = lambda *dims: pl.BlockSpec(dims, lambda i: (0,) * len(dims))
    return call(
        forward_body,
        (shape((CAP, CH, COLS)), shape((CH, DEEP), BF), shape((32, 8, COLS))),
        [
            SMEM,
            whole(4, 16, ROWS, LANES),
            whole(4, 16, ROWS, LANES),
            pl.BlockSpec((DEEP, 256), lambda i: (0, i)),
        ],
        grid=(4,),
        out_specs=(whole(CAP, CH, COLS), whole(CH, DEEP), whole(32, 8, COLS)),
        cost=6,
        room=24,
    )(live, mine, other, patch)


def to_row(value, spare):
    spare[...] = jnp.zeros(spare.shape, F32)
    spare[0:CH, :] = value
    return jnp.sum(jnp.transpose(spare[...]), axis=0, keepdims=True)


def norm_body(
    live_ref, stats, mixed, upstream, gain, bias, active, dshift, moments, message, sums, spare
):
    live = live_ref[0, 0]
    hot = one_hot()
    part, square, count = stats[:, 0, :], stats[:, 1, :], stats[:, 2, :]
    mean_row = jnp.sum(part, axis=0, keepdims=True) * (1.0 / POPULATION)
    offset = part / count - mean_row
    spread = jnp.sum(square + count * offset * offset, axis=0, keepdims=True)
    inverse_row = lax.rsqrt(spread * (1.0 / POPULATION) + 1e-05)
    moments[0] = from_groups(mean_row, hot)
    moments[1] = from_groups(inverse_row, hot)
    sums[...] = jnp.zeros(sums.shape, F32)

    def row(r, carry):
        alive = r < live
        for part in range(8):
            at = pl.ds(part * ROWS, ROWS)
            normed = (mixed[r, at, :] - moments[0, at, :]) * moments[1, at, :]
            shifted = normed * gain[at, :] + bias[at, :]
            gate = jax.nn.sigmoid(shifted)
            active[r, at, :] = jnp.where(alive, shifted * gate, 0.0).astype(BF)
            above = upstream[r, at, :].astype(F32)
            change = jnp.where(alive, above * gate * (1.0 + shifted * (1.0 - gate)), 0.0)
            dshift[r, at, :] = change
            sums[0, at, :] += change * normed
            sums[1, at, :] += change
        return carry

    lax.fori_loop(0, CAP, row, 0)
    gain_row = to_row(sums[0], spare)
    bias_row = to_row(sums[1], spare)
    line = lax.broadcasted_iota(jnp.int32, (8, 384), 0)
    note = jnp.where(line == 0, gain_row, bias_row)
    for tile in range(32):
        message[tile] = note[0:2]


def normalize(live, stats, mixed, upstream, gain, bias):
    return call(
        norm_body,
        (
            shape((CAP, CH, COLS), BF),
            shape((CAP, CH, COLS)),
            shape((2, CH, COLS)),
            shape((32, 2, 384)),
        ),
        [SMEM] + [VMEM] * 5,
        [pltpu.VMEM((2, CH, COLS), F32), pltpu.VMEM((384, COLS), F32)],
        out_specs=(VMEM,) * 4,
        cost=4,
    )(live, stats, mixed, upstream, gain, bias)


def to_column(row):
    return jnp.transpose(jnp.broadcast_to(row, (COLS, 384)))[:CH]


def grad_body(
    live_ref, notes, mixed, dshift, moments, gain, patch, pre, keep, send, riders, field
):
    step = pl.program_id(0)
    core = spot("core")

    @pl.when(step == 0)
    def _():
        live = live_ref[0, 0]
        hot = one_hot()
        totals = jnp.sum(notes[...], axis=0)
        gain_total = to_column(totals[0:1])
        bias_total = to_column(totals[1:2])
        lane = lax.broadcasted_iota(jnp.int32, (CH, COLS), 1)
        gain_high = gain_total.astype(BF).astype(F32)
        bias_high = bias_total.astype(BF).astype(F32)
        packed = jnp.where(lane == 0, gain_high, jnp.where(lane == 1, gain_total - gain_high, 0.0))
        packed = jnp.where(lane == 2, bias_high, packed)
        riders[...] = jnp.where(lane == 3, bias_total - bias_high, packed)
        share = 1.0 / POPULATION
        delta = from_groups(to_groups(bias_total * gain[...], hot) * share, hot)
        cross = from_groups(to_groups(gain_total * gain[...], hot) * share, hot)
        for r in range(CAP):
            normed = (mixed[r] - moments[0]) * moments[1]
            value = moments[1] * (dshift[r] * gain[...] - delta - normed * cross)
            value = jnp.where(r < live, value, 0.0).astype(BF)
            pre[r] = value
            field[:, r * COLS : (r + 1) * COLS] = value

    block = lax.dot_general(
        field[...], patch[...], (((1,), (1,)), ((), ())), preferred_element_type=F32
    )

    def write(target, side):
        for y in range(4):
            rows = block[side * 160 + y * ROWS : side * 160 + (y + 1) * ROWS]
            for local_frame in range(4):
                at = (local_frame // 2) * 384 + (local_frame % 2) * 128
                target[y, local_frame] = rows[:, at : at + LANES].astype(BF)

    @pl.when(core == 0)
    def _():
        write(keep, 0)
        write(send, 1)

    @pl.when(core == 1)
    def _():
        write(keep, 1)
        write(send, 0)


def gradients(live, notes, mixed, dshift, moments, gain, patch):
    whole = lambda *dims: pl.BlockSpec(dims, lambda i: (0,) * len(dims))
    halves = pl.BlockSpec((4, 4, ROWS, LANES), lambda i: (0, i, 0, 0))
    return call(
        grad_body,
        (
            shape((CAP, CH, COLS), BF),
            shape((4, 16, ROWS, LANES), BF),
            shape((4, 16, ROWS, LANES), BF),
            shape((CH, COLS)),
        ),
        [
            SMEM,
            whole(32, 2, 384),
            whole(CAP, CH, COLS),
            whole(CAP, CH, COLS),
            whole(2, CH, COLS),
            whole(CH, COLS),
            pl.BlockSpec((768, CAP * COLS), lambda i: (i, 0)),
        ],
        [pltpu.VMEM((CH, CAP * COLS), BF)],
        grid=(4,),
        out_specs=(whole(CAP, CH, COLS), halves, halves, whole(CH, COLS)),
        cost=7,
        room=24,
    )(live, notes, mixed, dshift, moments, gain, patch)


def quad_body(quads, riders, out):
    piece = spot("core") * 4 + spot("y")
    lane = lax.broadcasted_iota(jnp.int32, (ROWS, COLS), 1)
    ride = riders[pl.ds(pl.multiple_of(piece * ROWS, 8), ROWS), :]
    ride = jnp.where(spot("x") == 0, ride, 0.0)
    even = pltpu.roll(ride, SHARD - 128, 1)
    odd = pltpu.roll(ride, SHARD - 64, 1)
    for frame in range(16):
        total = quads[0, frame].astype(F32)
        for y in range(1, 4):
            total = total + quads[y, frame].astype(F32)
        first = SHARD - 128 if frame % 2 == 0 else SHARD - 64
        moved = even if frame % 2 == 0 else odd
        inside = (lane >= first) & (lane < first + 4)
        out[frame, :, 0:128] = total[:, :128].astype(BF)
        out[frame, :, 128:256] = jnp.where(inside, moved, total[:, 128:]).astype(BF)


def quad_sum(quads, riders):
    return call(
        quad_body, shape((16, ROWS, LANES), BF), [VMEM, VMEM], out_specs=VMEM
    )(quads, riders)


def frame_body(frames, out):
    total = frames[0].astype(F32)
    for frame in range(1, 16):
        total = total + frames[frame].astype(F32)
    first = SHARD + 64 * (spot("fsdp") % 2)
    lane = lax.broadcasted_iota(jnp.int32, (ROWS, LANES), 1)
    after = pltpu.roll(total, LANES - 1, 1)
    before = pltpu.roll(total, 1, 1)
    both = jnp.where((lane == first) | (lane == first + 2), total + after, total + before)
    high = both.astype(BF).astype(F32)
    riding = (lane >= first) & (lane < first + 4)
    leads = (lane == first) | (lane == first + 2)
    value = jnp.where(riding, jnp.where(leads, high, both - high), total).astype(BF)
    for tile in range(32):
        out[tile] = value


def frame_sum(frames):
    return call(frame_body, shape((32, ROWS, LANES), BF), [VMEM], out_specs=VMEM)(frames)


def adam_body(
    tiles, master, first, second, grad, weight_out, first_out, second_out, gain, bias, square
):
    for core in range(2):
        for y in range(4):
            total = tiles[y * 8 + core].astype(F32)
            for x in range(1, 4):
                total = total + tiles[y * 8 + x * 2 + core].astype(F32)
            at = (core * 4 + y) * ROWS
            square[at : at + ROWS, :] = total
    square[CH:, :] = jnp.zeros((64, LANES), F32)
    turned = jnp.transpose(square[...])[:, :CH] * SCALE
    odd = (spot("fsdp") % 2) == 1
    rows = jnp.where(odd, turned[64:256], turned[0:192])
    gain[...] = rows[SHARD : SHARD + 1] + rows[SHARD + 1 : SHARD + 2]
    bias[...] = rows[SHARD + 2 : SHARD + 3] + rows[SHARD + 3 : SHARD + 4]
    value = rows[:SHARD]
    grad[...] = value
    new_first = 0.9 * first[...] + 0.1 * value
    new_second = 0.999 * second[...] + 0.001 * value * value
    first_out[...] = new_first
    second_out[...] = new_second
    first_fix = new_first / (1.0 - 0.9**10)
    second_fix = new_second / (1.0 - 0.999**10)
    weight_out[...] = master[...] - 0.01 * first_fix / (jnp.sqrt(second_fix) + 1e-08)


def adam(tiles, master, first, second):
    return call(
        adam_body,
        (shape((SHARD, CH)),) * 4 + (shape((1, CH)),) * 2,
        [VMEM] * 4,
        [pltpu.VMEM((384, LANES), F32)],
        out_specs=(VMEM,) * 6,
    )(tiles, master, first, second)


def back_body(live_ref, weight, pre, above, below, out, field, total):
    live = live_ref[0, 0]

    def put(tap, r, value):
        field[tap, :, r * COLS : (r + 1) * COLS] = value.astype(BF)

    for slot in range(CAP + 2):
        store_taps(framed_row(slot, pre, above, below, live), put, slot, True)
    for tap in range(9):
        start = tap * CH
        parts = []
        while start < (tap + 1) * CH:
            frame = start // SHARD
            stop = min((frame + 1) * SHARD, (tap + 1) * CH)
            parts.append(weight[:, start + 12 * frame : stop + 12 * frame])
            start = stop
        left = jnp.concatenate(parts, axis=1)
        block = lax.dot_general(
            left, field[tap], (((0,), (0,)), ((), ())), preferred_element_type=F32
        )
        total[...] = block if tap == 0 else total[...] + block
    for r in range(CAP):
        value = total[:, r * COLS : (r + 1) * COLS]
        out[r] = jnp.where(r < live, value, 0.0).astype(BF)


def back(live, weight, pre, above, below):
    return call(
        back_body,
        shape((CAP, CH, COLS), BF),
        [SMEM] + [VMEM] * 4,
        [pltpu.VMEM((9, CH, CAP * COLS), BF), pltpu.VMEM((CH, CAP * COLS), F32)],
        out_specs=VMEM,
        cost=14,
        room=24,
    )(live, weight, pre, above, below)


def beside(first_row, last_row):
    count = 32
    ends = count - 1
    above = lax.ppermute(last_row, TILE, [(i, (i + 1) % count) for i in range(ends)])
    below = lax.ppermute(first_row, TILE, [((i + 1) % count, i) for i in range(ends)])
    return above, below


def gather_equal(value, axes, count):
    copies = jnp.broadcast_to(value, (count,) + value.shape)
    return lax.all_to_all(copies, axes, 0, 0)


def other_core(value):
    return lax.ppermute(value, "core", [(0, 1), (1, 0)])


def local(
    images, tile_rows, cotangent, master_weight, norm_gain, norm_bias, first_moment, second_moment
):
    live = tile_rows[0, 0]
    own = jnp.swapaxes(images[0, 0], 1, 2)
    upstream = jnp.swapaxes(cotangent[0, 0], 1, 2)
    along_z = lax.all_to_all(pack(master_weight), "fsdp", 0, 0)
    above, below = beside(own[0:1], lax.dynamic_slice_in_dim(own, live - 1, 1, 0))
    patch = patches(tile_rows, own, above, below)
    along_z, patch = lax.optimization_barrier((along_z, patch))
    mine = gather_equal(along_z, "y", 4)
    other = other_core(mine)
    mixed, weight, message = forward(tile_rows, mine, other, patch)
    stats = lax.all_to_all(message, TILE, 0, 0)
    gain = jnp.broadcast_to(norm_gain[:, None], (CH, COLS))
    bias = jnp.broadcast_to(norm_bias[:, None], (CH, COLS))
    active, dshift, moments, note = normalize(tile_rows, stats, mixed, upstream, gain, bias)
    notes = lax.all_to_all(note, TILE, 0, 0)
    pre, keep, send, riders = gradients(tile_rows, notes, mixed, dshift, moments, gain, patch)
    above_grad, below_grad = beside(pre[0:1], lax.dynamic_slice_in_dim(pre, live - 1, 1, 0))
    pair = (keep.astype(F32) + other_core(send).astype(F32)).astype(BF)
    quads = lax.all_to_all(pair, "y", 0, 0)
    frames = lax.all_to_all(quad_sum(quads, riders), "fsdp", 0, 0)
    image_grad = back(tile_rows, weight, pre, above_grad, below_grad)
    tiles = lax.all_to_all(frame_sum(frames), TILE, 0, 0)
    grad, new_weight, new_first, new_second, gain_grad, bias_grad = adam(
        tiles, master_weight, first_moment, second_moment
    )
    return (
        jnp.swapaxes(active, 1, 2)[None, None],
        jnp.swapaxes(image_grad, 1, 2)[None, None],
        grad,
        new_weight,
        new_first,
        new_second,
        gain_grad.reshape(CH),
        bias_grad.reshape(CH),
    )


def solution(mesh):
    fine = Mesh(mesh.devices.reshape(4, 4, 2, 16), ("y", "x", "core", "fsdp"))
    pixels = P("fsdp", TILE, None, None, None)
    rows = P("fsdp", None)
    return jax.shard_map(
        local,
        mesh=fine,
        in_specs=(pixels, P("fsdp", TILE), pixels, rows, P(), P(), rows, rows),
        out_specs=(pixels, pixels, rows, rows, rows, rows, P(), P()),
        check_vma=False,
    )
```

```python
import functools
import jax
import jax.numpy as jnp
from jax import lax
from jax.experimental import pallas as pl
from jax.experimental.pallas import tpu as pltpu
from jax.sharding import Mesh, PartitionSpec as P

TILE = ("y", "x", "core")
CH = 320
PER = 10
COLS = 128
CAP = 8
SHARD = 180
WIDE = 192
DEEP = 16 * WIDE
ROWS = 40
LANES = 256
POPULATION = 204800.0
SCALE = 327680.0 ** -0.5
BF = jnp.bfloat16
F32 = jnp.float32
VMEM = pl.BlockSpec(memory_space=pltpu.VMEM)
SMEM = pl.BlockSpec(memory_space=pltpu.SMEM)


def spot(name):
    return lax.axis_index(name)


def call(body, outs, ins, scratch=(), grid=None, cost=1, room=16, **more):
    if grid is not None:
        more["grid"] = grid
    return pl.pallas_call(
        body,
        out_shape=outs,
        in_specs=ins,
        scratch_shapes=list(scratch),
        compiler_params=pltpu.CompilerParams(vmem_limit_bytes=room << 20),
        cost_estimate=pl.CostEstimate(
            flops=cost * 1000000000, bytes_accessed=cost << 21, transcendentals=0
        ),
        **more,
    )


def shape(dims, kind=F32):
    return jax.ShapeDtypeStruct(dims, kind)


def compact(main, rest):
    left = lax.broadcasted_iota(jnp.int32, (8, COLS), 1) < 64
    tiles = [main(group) for group in range(5)]
    for low in (0, 2):
        tiles.append(jnp.where(left, rest(low, 0), rest(low + 1, 1)))
    tiles.append(jnp.where(left, rest(4, 0), 0.0))
    return tiles


def pack_body(weight, out, padded, turned, tight):
    padded[...] = jnp.zeros(padded.shape, F32)
    padded[0:SHARD, 0:CH] = weight[...]
    turned[...] = jnp.transpose(padded[...])
    piece = spot("core") * 4 + spot("y")
    rows = turned[pl.ds(pl.multiple_of(piece * ROWS, 8), ROWS), :]
    odd = (spot("fsdp") % 2) == 1

    def main(group):
        value = rows[group * 8 : group * 8 + 8, 0:128]
        return jnp.where(odd, pltpu.roll(value, 64, 1), value)

    def rest(group, side):
        value = rows[group * 8 : group * 8 + 8, 128:256]
        return pltpu.roll(value, 64, 1) if side else value

    for index, tile in enumerate(compact(main, rest)):
        tight[index * 8 : index * 8 + 8] = tile
    mine = tight[pl.ds(pl.multiple_of(spot("x") * 16, 8), 16), :].astype(BF)
    for frame in range(16):
        out[frame] = mine


def pack(weight):
    return call(
        pack_body,
        shape((16, 16, COLS), BF),
        [VMEM],
        [
            pltpu.VMEM((256, 384), F32),
            pltpu.VMEM((384, 256), F32),
            pltpu.VMEM((64, COLS), F32),
        ],
        out_specs=VMEM,
    )(weight)


def edge_body(live_ref, own, token, first_row, last_row):
    first_row[0] = own[0]
    last_row[0] = own[live_ref[0, 0] - 1]


def edges(live, own, token):
    return call(
        edge_body,
        (shape((1, CH, COLS), BF),) * 2,
        [SMEM, VMEM, pl.BlockSpec(memory_space=pl.ANY)],
        out_specs=(VMEM, VMEM),
    )(live, own, token)


def copies_body(value, out):
    for index in range(out.shape[0]):
        out[index] = value[...]


def copies(value, count):
    return call(
        copies_body, shape((count,) + value.shape, value.dtype), [VMEM], out_specs=VMEM
    )(value)


def store_taps(row, field, slot, negate):
    lane = lax.broadcasted_iota(jnp.int32, (CH, COLS), 1)
    for b in range(3):
        turn = (1 - b) if not negate else (b - 1)
        if turn == 0:
            moved = row
        elif turn == 1:
            moved = jnp.where(lane == 0, 0.0, pltpu.roll(row, 1, 1))
        else:
            moved = jnp.where(lane == COLS - 1, 0.0, pltpu.roll(row, COLS - 1, 1))
        for a in range(3):
            up = a if not negate else 2 - a
            r = slot - up
            if 0 <= r < CAP:
                field(3 * a + b, r, moved)


def framed_row(slot, own, above, below, live):
    if slot == 0:
        return above[0].astype(F32)
    base = own[slot - 1].astype(F32) if slot <= CAP else jnp.zeros((CH, COLS), F32)
    if slot == 1:
        return base
    under = below[0].astype(F32)
    return jnp.where(slot - 1 < live, base, jnp.where(slot - 1 == live, under, 0.0))


def patch_body(live_ref, own, above, below, out, wide):
    live = live_ref[0, 0]

    def put(tap, r, value):
        start = tap * CH
        while start < (tap + 1) * CH:
            frame = start // SHARD
            stop = min((frame + 1) * SHARD, (tap + 1) * CH)
            wide[r, start + 12 * frame : stop + 12 * frame, :] = value[
                start - tap * CH : stop - tap * CH
            ]
            start = stop

    for frame in range(16):
        first = frame * WIDE + SHARD
        wide[:, first : first + 12, :] = jnp.zeros((CAP, 12, COLS), F32)
    for slot in range(CAP + 2):
        store_taps(framed_row(slot, own, above, below, live), put, slot, False)
    for r in range(CAP):
        out[:, r * COLS : (r + 1) * COLS] = wide[r].astype(BF)


def patches(live, own, above, below):
    return call(
        patch_body,
        shape((DEEP, CAP * COLS), BF),
        [SMEM, VMEM, VMEM, VMEM],
        [pltpu.VMEM((CAP, DEEP, COLS), F32)],
        out_specs=VMEM,
        cost=8,
        room=30,
    )(live, own, above, below)


def one_hot():
    channel = lax.broadcasted_iota(jnp.int32, (CH, COLS), 0)
    lane = lax.broadcasted_iota(jnp.int32, (CH, COLS), 1) * PER
    return jnp.where((channel >= lane) & (channel < lane + PER), 1.0, 0.0)


def to_groups(column, hot):
    return jnp.sum(column * hot, axis=0, keepdims=True)


def from_groups(row, hot):
    return jnp.broadcast_to(jnp.sum(row * hot, axis=1, keepdims=True), (CH, COLS))


def forward_body(live_ref, mine, other, patch, mixed, weight, message, held, arrived):
    step = pl.program_id(0)

    def block_copy(index):
        return pltpu.make_async_copy(
            patch.at[:, index * 256 : (index + 1) * 256], held.at[index], arrived.at[index]
        )

    @pl.when(step == 0)
    def _():
        for index in range(4):
            block_copy(index).start()
        left = lax.broadcasted_iota(jnp.int32, (8, COLS), 1) < 64
        for half, source in ((0, mine), (1, other)):
            side = (spot("core") + half) % 2
            for y in range(4):
                base = pl.multiple_of(side * 160 + y * ROWS, 8)
                for pair in range(8):
                    at = pair * 384

                    def tile(frame, index):
                        row = (index % 2) * 8
                        value = source[y * 4 + index // 2, 2 * pair + frame, row : row + 8, :]
                        return value.astype(F32)

                    even = [tile(0, index) for index in range(8)]
                    odd = [tile(1, index) for index in range(8)]
                    first, middle, last = [], [], []
                    for group in range(5):
                        rest = [even[5 + group // 2], odd[5 + group // 2]]
                        turn = 1 - group % 2
                        rest[turn] = pltpu.roll(rest[turn], 64, 1)
                        first.append(even[group])
                        middle.append(jnp.where(left, rest[0], odd[group]))
                        last.append(jnp.where(left, odd[group], rest[1]))
                    for place, parts in ((0, first), (128, middle), (256, last)):
                        weight[pl.ds(base, ROWS), at + place : at + place + 128] = (
                            jnp.concatenate(parts, axis=0).astype(BF)
                        )

    for index in range(4):

        @pl.when(step == index)
        def _():
            block_copy(index).wait()

    block = jnp.dot(weight[...], held[step], preferred_element_type=F32)
    mixed[2 * step] = block[:, :128]
    mixed[2 * step + 1] = block[:, 128:]

    @pl.when(step == 3)
    def _():
        live = live_ref[0, 0]
        hot = one_hot()
        total = jnp.zeros((CH, COLS), F32)
        for r in range(CAP):
            total = total + jnp.where(r < live, mixed[r], 0.0)
        column = jnp.broadcast_to(jnp.sum(total, axis=1, keepdims=True), (CH, COLS))
        sums = to_groups(column, hot)
        count = live.astype(F32) * (COLS * PER)
        mean = from_groups(sums / count, hot)
        square = jnp.zeros((CH, COLS), F32)
        for r in range(CAP):
            away = mixed[r] - mean
            square = square + jnp.where(r < live, away * away, 0.0)
        column = jnp.broadcast_to(jnp.sum(square, axis=1, keepdims=True), (CH, COLS))
        squares = to_groups(column, hot)
        line = lax.broadcasted_iota(jnp.int32, (8, COLS), 0)
        note = jnp.where(line == 0, sums, jnp.where(line == 1, squares, count))
        for tile in range(32):
            message[tile] = note


def forward(live, mine, other, patch):
    whole = lambda *dims: pl.BlockSpec(dims, lambda i: (0,) * len(dims))
    return call(
        forward_body,
        (shape((CAP, CH, COLS)), shape((CH, DEEP), BF), shape((32, 8, COLS))),
        [
            SMEM,
            whole(16, 16, 16, COLS),
            whole(16, 16, 16, COLS),
            pl.BlockSpec(memory_space=pltpu.HBM),
        ],
        [pltpu.VMEM((4, DEEP, 256), BF), pltpu.SemaphoreType.DMA((4,))],
        grid=(4,),
        out_specs=(whole(CAP, CH, COLS), whole(CH, DEEP), whole(32, 8, COLS)),
        cost=6,
        room=24,
    )(live, mine, other, patch)


def to_row(value, spare):
    spare[...] = jnp.zeros(spare.shape, F32)
    spare[0:CH, :] = value
    return jnp.sum(jnp.transpose(spare[...]), axis=0, keepdims=True)


def norm_body(
    live_ref, stats, mixed, upstream, gain, bias, active, dshift, moments, message, sums, spare
):
    live = live_ref[0, 0]
    hot = one_hot()
    part, square, count = stats[:, 0, :], stats[:, 1, :], stats[:, 2, :]
    mean_row = jnp.sum(part, axis=0, keepdims=True) * (1.0 / POPULATION)
    offset = part / count - mean_row
    spread = jnp.sum(square + count * offset * offset, axis=0, keepdims=True)
    inverse_row = lax.rsqrt(spread * (1.0 / POPULATION) + 1e-05)
    moments[0] = from_groups(mean_row, hot)
    moments[1] = from_groups(inverse_row, hot)
    sums[...] = jnp.zeros(sums.shape, F32)

    def row(r, carry):
        alive = r < live
        for part in range(8):
            at = pl.ds(part * ROWS, ROWS)
            normed = (mixed[r, at, :] - moments[0, at, :]) * moments[1, at, :]
            shifted = normed * gain[at, :] + bias[at, :]
            gate = jax.nn.sigmoid(shifted)
            active[r, at, :] = jnp.where(alive, shifted * gate, 0.0).astype(BF)
            above = upstream[r, at, :].astype(F32)
            change = jnp.where(alive, above * gate * (1.0 + shifted * (1.0 - gate)), 0.0)
            dshift[r, at, :] = change
            sums[0, at, :] += change * normed
            sums[1, at, :] += change
        return carry

    lax.fori_loop(0, CAP, row, 0)
    gain_row = to_row(sums[0], spare)
    bias_row = to_row(sums[1], spare)
    line = lax.broadcasted_iota(jnp.int32, (8, 384), 0)
    note = jnp.where(line == 0, gain_row, bias_row)
    for tile in range(32):
        message[tile] = note[0:2]


def normalize(live, stats, mixed, upstream, gain, bias):
    return call(
        norm_body,
        (
            shape((CAP, CH, COLS), BF),
            shape((CAP, CH, COLS)),
            shape((2, CH, COLS)),
            shape((32, 2, 384)),
        ),
        [SMEM] + [VMEM] * 5,
        [pltpu.VMEM((2, CH, COLS), F32), pltpu.VMEM((384, COLS), F32)],
        out_specs=(VMEM,) * 4,
        cost=4,
    )(live, stats, mixed, upstream, gain, bias)


def to_column(row):
    return jnp.transpose(jnp.broadcast_to(row, (COLS, 384)))[:CH]


def grad_body(
    live_ref,
    notes,
    mixed,
    dshift,
    moments,
    gain,
    patch,
    pre,
    keep,
    send,
    riders,
    first_row,
    last_row,
    field,
    held,
    arrived,
):
    step = pl.program_id(0)
    core = spot("core")

    def block_copy(index):
        return pltpu.make_async_copy(
            patch.at[index * 768 : (index + 1) * 768], held.at[index], arrived.at[index]
        )

    @pl.when(step == 0)
    def _():
        for index in range(4):
            block_copy(index).start()
        live = live_ref[0, 0]
        hot = one_hot()
        totals = jnp.sum(notes[...], axis=0)
        gain_total = to_column(totals[0:1])
        bias_total = to_column(totals[1:2])
        lane = lax.broadcasted_iota(jnp.int32, (CH, COLS), 1)
        gain_high = gain_total.astype(BF).astype(F32)
        bias_high = bias_total.astype(BF).astype(F32)
        packed = jnp.where(lane == 0, gain_high, jnp.where(lane == 1, gain_total - gain_high, 0.0))
        packed = jnp.where(lane == 2, bias_high, packed)
        riders[...] = jnp.where(lane == 3, bias_total - bias_high, packed)
        share = 1.0 / POPULATION
        delta = from_groups(to_groups(bias_total * gain[...], hot) * share, hot)
        cross = from_groups(to_groups(gain_total * gain[...], hot) * share, hot)
        for r in range(CAP):
            normed = (mixed[r] - moments[0]) * moments[1]
            value = moments[1] * (dshift[r] * gain[...] - delta - normed * cross)
            value = jnp.where(r < live, value, 0.0).astype(BF)
            pre[r] = value
            field[:, r * COLS : (r + 1) * COLS] = value
        first_row[0] = pre[0]
        last_row[0] = pre[live - 1]

    for index in range(4):

        @pl.when(step == index)
        def _():
            block_copy(index).wait()

    block = lax.dot_general(
        field[...], held[step], (((1,), (1,)), ((), ())), preferred_element_type=F32
    )

    left = lax.broadcasted_iota(jnp.int32, (8, COLS), 1) < 64

    def write(target, side):
        for y in range(4):
            base = side * 160 + y * ROWS
            for frame in range(4):
                at = (frame // 2) * 384 + (frame % 2) * 128
                odd = frame % 2

                def part(group, offset):
                    row = base + group * 8
                    return block[row : row + 8, at + offset : at + offset + 128]

                def main(group):
                    if odd:
                        return jnp.where(left, part(group, 128), part(group, 0))
                    return part(group, 0)

                def rest(group, place):
                    value = part(group, 128)
                    return value if place == odd else pltpu.roll(value, 64, 1)

                tiles = compact(main, rest)
                for x in range(4):
                    target[y * 4 + x, frame] = jnp.concatenate(
                        tiles[2 * x : 2 * x + 2], axis=0
                    ).astype(BF)

    @pl.when(core == 0)
    def _():
        write(keep, 0)
        write(send, 1)

    @pl.when(core == 1)
    def _():
        write(keep, 1)
        write(send, 0)


def gradients(live, notes, mixed, dshift, moments, gain, patch):
    whole = lambda *dims: pl.BlockSpec(dims, lambda i: (0,) * len(dims))
    halves = pl.BlockSpec((16, 4, 16, COLS), lambda i: (0, i, 0, 0))
    return call(
        grad_body,
        (
            shape((CAP, CH, COLS), BF),
            shape((16, 16, 16, COLS), BF),
            shape((16, 16, 16, COLS), BF),
            shape((CH, COLS)),
            shape((1, CH, COLS), BF),
            shape((1, CH, COLS), BF),
        ),
        [
            SMEM,
            whole(32, 2, 384),
            whole(CAP, CH, COLS),
            whole(CAP, CH, COLS),
            whole(2, CH, COLS),
            whole(CH, COLS),
            pl.BlockSpec(memory_space=pltpu.HBM),
        ],
        [
            pltpu.VMEM((CH, CAP * COLS), BF),
            pltpu.VMEM((4, 768, CAP * COLS), BF),
            pltpu.SemaphoreType.DMA((4,)),
        ],
        grid=(4,),
        out_specs=(
            whole(CAP, CH, COLS),
            halves,
            halves,
            whole(CH, COLS),
            whole(1, CH, COLS),
            whole(1, CH, COLS),
        ),
        cost=7,
        room=24,
    )(live, notes, mixed, dshift, moments, gain, patch)


def add_body(keep, passed, out):
    for index in range(16):
        out[index] = (keep[index].astype(F32) + passed[index].astype(F32)).astype(BF)


def add_pair(keep, passed):
    return call(
        add_body, shape((16, 16, 16, COLS), BF), [VMEM, VMEM], out_specs=VMEM
    )(keep, passed)


def plane_body(parts, riders, out):
    piece = spot("core") * 4 + spot("y")
    ride = jnp.zeros((8, COLS), F32)
    for group in range(5):
        at = pl.multiple_of(piece * ROWS + group * 8, 8)
        ride = ride + pltpu.roll(riders[pl.ds(at, 8), :], 64 + 4 * group, 1)
    ride = jnp.where(spot("x") == 3, ride, 0.0)
    ride = jnp.concatenate([jnp.zeros((8, COLS), F32), ride], axis=0)
    for frame in range(16):
        total = parts[0, frame].astype(F32)
        for part in range(1, 16):
            total = total + parts[part, frame].astype(F32)
        out[frame] = (total + ride).astype(BF)


def plane_sum(parts, riders):
    return call(
        plane_body, shape((16, 16, COLS), BF), [VMEM, VMEM], out_specs=VMEM
    )(parts, riders)


def frame_body(frames, out):
    total = frames[0].astype(F32)
    for frame in range(1, 16):
        total = total + frames[frame].astype(F32)
    lane = lax.broadcasted_iota(jnp.int32, (16, COLS), 1)
    row = lax.broadcasted_iota(jnp.int32, (16, COLS), 0)
    leads = lane % 2 == 0
    both = total + jnp.where(leads, pltpu.roll(total, COLS - 1, 1), pltpu.roll(total, 1, 1))
    high = both.astype(BF).astype(F32)
    riding = (lane >= 64) & (row >= 8) & (spot("x") == 3)
    value = jnp.where(riding, jnp.where(leads, high, both - high), total).astype(BF)
    for tile in range(32):
        out[tile] = value


def frame_sum(frames):
    return call(frame_body, shape((32, 16, COLS), BF), [VMEM], out_specs=VMEM)(frames)


def adam_body(
    tiles, master, first, second, grad, weight_out, first_out, second_out, gain, bias, square
):
    odd = (spot("fsdp") % 2) == 1
    lane = lax.broadcasted_iota(jnp.int32, (8, COLS), 1)
    for core in range(2):
        for y in range(4):
            part = [
                tiles[y * 8 + (index // 2) * 2 + core, (index % 2) * 8 : (index % 2) * 8 + 8, :]
                for index in range(8)
            ]
            part = [value.astype(F32) for value in part]
            for group in range(5):
                at = (core * 4 + y) * ROWS + group * 8
                main = part[group]
                rest = part[5 + group // 2]
                if group % 2:
                    rest = pltpu.roll(rest, 64, 1)
                ride = pltpu.roll(part[7], COLS - 4 * group, 1)
                square[at : at + 8, 0:128] = jnp.where(odd, pltpu.roll(main, 64, 1), main)
                square[at : at + 8, 128:256] = jnp.where(lane < 64, rest, ride)
    square[CH:, :] = jnp.zeros((64, LANES), F32)
    turned = jnp.transpose(square[...])[:, :CH] * SCALE
    gain[...] = (turned[192:193] + turned[193:194])[0]
    bias[...] = (turned[194:195] + turned[195:196])[0]
    value = turned[:SHARD]
    grad[...] = value
    new_first = 0.9 * first[...] + 0.1 * value
    new_second = 0.999 * second[...] + 0.001 * value * value
    first_out[...] = new_first
    second_out[...] = new_second
    first_fix = new_first / (1.0 - 0.9**10)
    second_fix = new_second / (1.0 - 0.999**10)
    weight_out[...] = master[...] - 0.01 * first_fix / (jnp.sqrt(second_fix) + 1e-08)


def adam(tiles, master, first, second):
    return call(
        adam_body,
        (shape((SHARD, CH)),) * 4 + (shape((CH,)),) * 2,
        [VMEM] * 4,
        [pltpu.VMEM((384, LANES), F32)],
        out_specs=(VMEM,) * 6,
    )(tiles, master, first, second)


def back_body(live_ref, weight, pre, above, below, out, field, total):
    live = live_ref[0, 0]

    def put(tap, r, value):
        field[tap, :, r * COLS : (r + 1) * COLS] = value.astype(BF)

    for slot in range(CAP + 2):
        store_taps(framed_row(slot, pre, above, below, live), put, slot, True)
    for tap in range(9):
        start = tap * CH
        parts = []
        while start < (tap + 1) * CH:
            frame = start // SHARD
            stop = min((frame + 1) * SHARD, (tap + 1) * CH)
            parts.append(weight[:, start + 12 * frame : stop + 12 * frame])
            start = stop
        left = jnp.concatenate(parts, axis=1)
        block = lax.dot_general(
            left, field[tap], (((0,), (0,)), ((), ())), preferred_element_type=F32
        )
        total[...] = block if tap == 0 else total[...] + block
    for r in range(CAP):
        value = total[:, r * COLS : (r + 1) * COLS]
        out[r] = jnp.where(r < live, value, 0.0).astype(BF)


def back(live, weight, pre, above, below):
    return call(
        back_body,
        shape((CAP, CH, COLS), BF),
        [SMEM] + [VMEM] * 4,
        [pltpu.VMEM((9, CH, CAP * COLS), BF), pltpu.VMEM((CH, CAP * COLS), F32)],
        out_specs=VMEM,
        cost=14,
        room=24,
    )(live, weight, pre, above, below)


def beside(first_row, last_row):
    count = 32
    ends = count - 1
    above = lax.ppermute(last_row, TILE, [(i, (i + 1) % count) for i in range(ends)])
    below = lax.ppermute(first_row, TILE, [((i + 1) % count, i) for i in range(ends)])
    return above, below


def other_core(value):
    return lax.ppermute(value, "core", [(0, 1), (1, 0)])


def local(
    images, tile_rows, cotangent, master_weight, norm_gain, norm_bias, first_moment, second_moment
):
    own = jnp.swapaxes(images[0, 0], 1, 2)
    upstream = jnp.swapaxes(cotangent[0, 0], 1, 2)
    packed = pack(master_weight)
    along_z = lax.all_to_all(packed, "fsdp", 0, 0)
    above, below = beside(*edges(tile_rows, own, packed))
    patch = patches(tile_rows, own, above, below)
    patch = pltpu.with_memory_space_constraint(patch, pltpu.HBM)
    along_z, patch = lax.optimization_barrier((along_z, patch))
    mine = lax.all_to_all(copies(along_z, 16), ("y", "x"), 0, 0)
    other = other_core(mine)
    mixed, weight, message = forward(tile_rows, mine, other, patch)
    stats = lax.all_to_all(message, TILE, 0, 0)
    gain = jnp.broadcast_to(norm_gain[:, None], (CH, COLS))
    bias = jnp.broadcast_to(norm_bias[:, None], (CH, COLS))
    active, dshift, moments, note = normalize(tile_rows, stats, mixed, upstream, gain, bias)
    notes = lax.all_to_all(note, TILE, 0, 0)
    pre, keep, send, riders, pre_first, pre_last = gradients(
        tile_rows, notes, mixed, dshift, moments, gain, patch
    )
    above_grad, below_grad = beside(pre_first, pre_last)
    parts = lax.all_to_all(add_pair(keep, other_core(send)), ("y", "x"), 0, 0)
    frames = lax.all_to_all(plane_sum(parts, riders), "fsdp", 0, 0)
    image_grad = back(tile_rows, weight, pre, above_grad, below_grad)
    tiles = lax.all_to_all(frame_sum(frames), TILE, 0, 0)
    grad, new_weight, new_first, new_second, gain_grad, bias_grad = adam(
        tiles, master_weight, first_moment, second_moment
    )
    return (
        jnp.swapaxes(active, 1, 2)[None, None],
        jnp.swapaxes(image_grad, 1, 2)[None, None],
        grad,
        new_weight,
        new_first,
        new_second,
        gain_grad,
        bias_grad,
    )


def solution(mesh):
    fine = Mesh(mesh.devices.reshape(4, 4, 2, 16), ("y", "x", "core", "fsdp"))
    pixels = P("fsdp", TILE, None, None, None)
    rows = P("fsdp", None)
    return jax.shard_map(
        local,
        mesh=fine,
        in_specs=(pixels, P("fsdp", TILE), pixels, rows, P(), P(), rows, rows),
        out_specs=(pixels, pixels, rows, rows, rows, rows, P(), P()),
        check_vma=False,
    )
```

```python
import functools
import jax
import jax.numpy as jnp
from jax import lax
from jax.experimental import pallas as pl
from jax.experimental.pallas import tpu as pltpu
from jax.sharding import Mesh, PartitionSpec as P

TILE = ("y", "x", "core")
CH = 320
PER = 10
COLS = 128
CAP = 8
SHARD = 180
WIDE = 192
DEEP = 16 * WIDE
ROWS = 40
LANES = 256
POPULATION = 204800.0
SCALE = 327680.0 ** -0.5
BF = jnp.bfloat16
F32 = jnp.float32
VMEM = pl.BlockSpec(memory_space=pltpu.VMEM)
SMEM = pl.BlockSpec(memory_space=pltpu.SMEM)


def spot(name):
    return lax.axis_index(name)


def call(body, outs, ins, scratch=(), grid=None, cost=1, room=16, **more):
    if grid is not None:
        more["grid"] = grid
    return pl.pallas_call(
        body,
        out_shape=outs,
        in_specs=ins,
        scratch_shapes=list(scratch),
        compiler_params=pltpu.CompilerParams(vmem_limit_bytes=room << 20),
        cost_estimate=pl.CostEstimate(
            flops=cost * 1000000000, bytes_accessed=cost << 21, transcendentals=0
        ),
        **more,
    )


def shape(dims, kind=F32):
    return jax.ShapeDtypeStruct(dims, kind)


def compact(main, rest):
    left = lax.broadcasted_iota(jnp.int32, (8, COLS), 1) < 64
    tiles = [main(group) for group in range(5)]
    for low in (0, 2):
        tiles.append(jnp.where(left, rest(low, 0), rest(low + 1, 1)))
    tiles.append(jnp.where(left, rest(4, 0), 0.0))
    return tiles


def pack_body(weight, out, padded, turned, tight):
    padded[...] = jnp.zeros(padded.shape, F32)
    padded[0:SHARD, 0:CH] = weight[...]
    turned[...] = jnp.transpose(padded[...])
    piece = spot("core") * 4 + spot("y")
    rows = turned[pl.ds(pl.multiple_of(piece * ROWS, 8), ROWS), :]
    odd = (spot("fsdp") % 2) == 1

    def main(group):
        value = rows[group * 8 : group * 8 + 8, 0:128]
        return jnp.where(odd, pltpu.roll(value, 64, 1), value)

    def rest(group, side):
        value = rows[group * 8 : group * 8 + 8, 128:256]
        return pltpu.roll(value, 64, 1) if side else value

    for index, tile in enumerate(compact(main, rest)):
        tight[index * 8 : index * 8 + 8] = tile
    mine = tight[pl.ds(pl.multiple_of(spot("x") * 16, 8), 16), :].astype(BF)
    for frame in range(16):
        out[frame] = mine


def pack(weight):
    return call(
        pack_body,
        shape((16, 16, COLS), BF),
        [VMEM],
        [
            pltpu.VMEM((256, 384), F32),
            pltpu.VMEM((384, 256), F32),
            pltpu.VMEM((64, COLS), F32),
        ],
        out_specs=VMEM,
    )(weight)


def edge_body(live_ref, own, token, first_row, last_row):
    first_row[0] = own[0]
    last_row[0] = own[live_ref[0, 0] - 1]


def edges(live, own, token):
    return call(
        edge_body,
        (shape((1, CH, COLS), BF),) * 2,
        [SMEM, VMEM, pl.BlockSpec(memory_space=pl.ANY)],
        out_specs=(VMEM, VMEM),
    )(live, own, token)


def copies_body(value, out):
    for index in range(out.shape[0]):
        out[index] = value[...]


def copies(value, count):
    return call(
        copies_body, shape((count,) + value.shape, value.dtype), [VMEM], out_specs=VMEM
    )(value)


def store_taps(row, field, slot, negate):
    lane = lax.broadcasted_iota(jnp.int32, (CH, COLS), 1)
    for b in range(3):
        turn = (1 - b) if not negate else (b - 1)
        if turn == 0:
            moved = row
        elif turn == 1:
            moved = jnp.where(lane == 0, 0.0, pltpu.roll(row, 1, 1))
        else:
            moved = jnp.where(lane == COLS - 1, 0.0, pltpu.roll(row, COLS - 1, 1))
        for a in range(3):
            up = a if not negate else 2 - a
            r = slot - up
            if 0 <= r < CAP:
                field(3 * a + b, r, moved)


def framed_row(slot, own, above, below, live):
    if slot == 0:
        return above[0].astype(F32)
    base = own[slot - 1].astype(F32) if slot <= CAP else jnp.zeros((CH, COLS), F32)
    if slot == 1:
        return base
    under = below[0].astype(F32)
    return jnp.where(slot - 1 < live, base, jnp.where(slot - 1 == live, under, 0.0))


def patch_body(live_ref, own, above, below, out, wide):
    live = live_ref[0, 0]

    def put(tap, r, value):
        start = tap * CH
        while start < (tap + 1) * CH:
            frame = start // SHARD
            stop = min((frame + 1) * SHARD, (tap + 1) * CH)
            wide[r, start + 12 * frame : stop + 12 * frame, :] = value[
                start - tap * CH : stop - tap * CH
            ]
            start = stop

    for frame in range(16):
        first = frame * WIDE + SHARD
        wide[:, first : first + 12, :] = jnp.zeros((CAP, 12, COLS), F32)
    for slot in range(CAP + 2):
        store_taps(framed_row(slot, own, above, below, live), put, slot, False)
    for r in range(CAP):
        out[:, r * COLS : (r + 1) * COLS] = wide[r].astype(BF)


def patches(live, own, above, below):
    return call(
        patch_body,
        shape((DEEP, CAP * COLS), BF),
        [SMEM, VMEM, VMEM, VMEM],
        [pltpu.VMEM((CAP, DEEP, COLS), F32)],
        out_specs=VMEM,
        cost=1,
        room=30,
    )(live, own, above, below)


def one_hot():
    channel = lax.broadcasted_iota(jnp.int32, (CH, COLS), 0)
    lane = lax.broadcasted_iota(jnp.int32, (CH, COLS), 1) * PER
    return jnp.where((channel >= lane) & (channel < lane + PER), 1.0, 0.0)


def to_groups(column, hot):
    return jnp.sum(column * hot, axis=0, keepdims=True)


def from_groups(row, hot):
    return jnp.broadcast_to(jnp.sum(row * hot, axis=1, keepdims=True), (CH, COLS))


def forward_body(live_ref, mine, other, patch, mixed, weight, message, held, arrived):
    step = pl.program_id(0)

    def block_copy(index):
        return pltpu.make_async_copy(
            patch.at[:, index * 256 : (index + 1) * 256], held.at[index], arrived.at[index]
        )

    @pl.when(step == 0)
    def _():
        block_copy(0).start()
        block_copy(1).start()
        left = lax.broadcasted_iota(jnp.int32, (8, COLS), 1) < 64
        for half, source in ((0, mine), (1, other)):
            side = (spot("core") + half) % 2
            for y in range(4):
                base = pl.multiple_of(side * 160 + y * ROWS, 8)
                for pair in range(8):
                    at = pair * 384

                    def tile(frame, index):
                        row = (index % 2) * 8
                        value = source[y * 4 + index // 2, 2 * pair + frame, row : row + 8, :]
                        return value.astype(F32)

                    even = [tile(0, index) for index in range(8)]
                    odd = [tile(1, index) for index in range(8)]
                    first, middle, last = [], [], []
                    for group in range(5):
                        rest = [even[5 + group // 2], odd[5 + group // 2]]
                        turn = 1 - group % 2
                        rest[turn] = pltpu.roll(rest[turn], 64, 1)
                        first.append(even[group])
                        middle.append(jnp.where(left, rest[0], odd[group]))
                        last.append(jnp.where(left, odd[group], rest[1]))
                    for place, parts in ((0, first), (128, middle), (256, last)):
                        weight[pl.ds(base, ROWS), at + place : at + place + 128] = (
                            jnp.concatenate(parts, axis=0).astype(BF)
                        )

    for index in range(4):

        @pl.when(step == index)
        def _():
            block_copy(index).wait()
            if index < 2:
                block_copy(index + 2).start()

    block = jnp.dot(weight[...], held[step], preferred_element_type=F32)
    mixed[2 * step] = block[:, :128]
    mixed[2 * step + 1] = block[:, 128:]

    @pl.when(step == 3)
    def _():
        live = live_ref[0, 0]
        hot = one_hot()
        total = jnp.zeros((CH, COLS), F32)
        for r in range(CAP):
            total = total + jnp.where(r < live, mixed[r], 0.0)
        column = jnp.broadcast_to(jnp.sum(total, axis=1, keepdims=True), (CH, COLS))
        sums = to_groups(column, hot)
        count = live.astype(F32) * (COLS * PER)
        mean = from_groups(sums / count, hot)
        square = jnp.zeros((CH, COLS), F32)
        for r in range(CAP):
            away = mixed[r] - mean
            square = square + jnp.where(r < live, away * away, 0.0)
        column = jnp.broadcast_to(jnp.sum(square, axis=1, keepdims=True), (CH, COLS))
        squares = to_groups(column, hot)
        line = lax.broadcasted_iota(jnp.int32, (8, COLS), 0)
        note = jnp.where(line == 0, sums, jnp.where(line == 1, squares, count))
        for tile in range(32):
            message[tile] = note


def forward(live, mine, other, patch):
    whole = lambda *dims: pl.BlockSpec(dims, lambda i: (0,) * len(dims))
    return call(
        forward_body,
        (shape((CAP, CH, COLS)), shape((CH, DEEP), BF), shape((32, 8, COLS))),
        [
            SMEM,
            whole(16, 16, 16, COLS),
            whole(16, 16, 16, COLS),
            pl.BlockSpec(memory_space=pltpu.HBM),
        ],
        [pltpu.VMEM((4, DEEP, 256), BF), pltpu.SemaphoreType.DMA((4,))],
        grid=(4,),
        out_specs=(whole(CAP, CH, COLS), whole(CH, DEEP), whole(32, 8, COLS)),
        cost=6,
        room=24,
    )(live, mine, other, patch)


def to_row(value, spare):
    spare[...] = jnp.zeros(spare.shape, F32)
    spare[0:CH, :] = value
    return jnp.sum(jnp.transpose(spare[...]), axis=0, keepdims=True)


def norm_body(
    live_ref, stats, mixed, upstream, gain, bias, active, dshift, moments, message, sums, spare
):
    live = live_ref[0, 0]
    hot = one_hot()
    part, square, count = stats[:, 0, :], stats[:, 1, :], stats[:, 2, :]
    mean_row = jnp.sum(part, axis=0, keepdims=True) * (1.0 / POPULATION)
    offset = part / count - mean_row
    spread = jnp.sum(square + count * offset * offset, axis=0, keepdims=True)
    inverse_row = lax.rsqrt(spread * (1.0 / POPULATION) + 1e-05)
    moments[0] = from_groups(mean_row, hot)
    moments[1] = from_groups(inverse_row, hot)
    sums[...] = jnp.zeros(sums.shape, F32)

    def row(r, carry):
        alive = r < live
        for part in range(8):
            at = pl.ds(part * ROWS, ROWS)
            normed = (mixed[r, at, :] - moments[0, at, :]) * moments[1, at, :]
            shifted = normed * gain[at, :] + bias[at, :]
            gate = jax.nn.sigmoid(shifted)
            active[r, at, :] = jnp.where(alive, shifted * gate, 0.0).astype(BF)
            above = upstream[r, at, :].astype(F32)
            change = jnp.where(alive, above * gate * (1.0 + shifted * (1.0 - gate)), 0.0)
            dshift[r, at, :] = change
            sums[0, at, :] += change * normed
            sums[1, at, :] += change
        return carry

    lax.fori_loop(0, CAP, row, 0)
    gain_row = to_row(sums[0], spare)
    bias_row = to_row(sums[1], spare)
    line = lax.broadcasted_iota(jnp.int32, (8, 384), 0)
    note = jnp.where(line == 0, gain_row, bias_row)
    for tile in range(32):
        message[tile] = note[0:2]


def normalize(live, stats, mixed, upstream, gain, bias):
    return call(
        norm_body,
        (
            shape((CAP, CH, COLS), BF),
            shape((CAP, CH, COLS)),
            shape((2, CH, COLS)),
            shape((32, 2, 384)),
        ),
        [SMEM] + [VMEM] * 5,
        [pltpu.VMEM((2, CH, COLS), F32), pltpu.VMEM((384, COLS), F32)],
        out_specs=(VMEM,) * 4,
        cost=4,
    )(live, stats, mixed, upstream, gain, bias)


def to_column(row):
    return jnp.transpose(jnp.broadcast_to(row, (COLS, 384)))[:CH]


def grad_body(
    live_ref,
    notes,
    mixed,
    dshift,
    moments,
    gain,
    patch,
    pre,
    keep,
    send,
    riders,
    first_row,
    last_row,
    field,
    held,
    arrived,
):
    step = pl.program_id(0)
    core = spot("core")

    def block_copy(index):
        return pltpu.make_async_copy(
            patch.at[index * 768 : (index + 1) * 768], held.at[index], arrived.at[index]
        )

    @pl.when(step == 0)
    def _():
        block_copy(0).start()
        block_copy(1).start()
        live = live_ref[0, 0]
        hot = one_hot()
        totals = jnp.sum(notes[...], axis=0)
        gain_total = to_column(totals[0:1])
        bias_total = to_column(totals[1:2])
        lane = lax.broadcasted_iota(jnp.int32, (CH, COLS), 1)
        gain_high = gain_total.astype(BF).astype(F32)
        bias_high = bias_total.astype(BF).astype(F32)
        packed = jnp.where(lane == 0, gain_high, jnp.where(lane == 1, gain_total - gain_high, 0.0))
        packed = jnp.where(lane == 2, bias_high, packed)
        riders[...] = jnp.where(lane == 3, bias_total - bias_high, packed)
        share = 1.0 / POPULATION
        delta = from_groups(to_groups(bias_total * gain[...], hot) * share, hot)
        cross = from_groups(to_groups(gain_total * gain[...], hot) * share, hot)
        for r in range(CAP):
            normed = (mixed[r] - moments[0]) * moments[1]
            value = moments[1] * (dshift[r] * gain[...] - delta - normed * cross)
            value = jnp.where(r < live, value, 0.0).astype(BF)
            pre[r] = value
            field[:, r * COLS : (r + 1) * COLS] = value
        first_row[0] = pre[0]
        last_row[0] = pre[live - 1]

    for index in range(4):

        @pl.when(step == index)
        def _():
            block_copy(index).wait()
            if index < 2:
                block_copy(index + 2).start()

    block = lax.dot_general(
        field[...], held[step], (((1,), (1,)), ((), ())), preferred_element_type=F32
    )

    left = lax.broadcasted_iota(jnp.int32, (8, COLS), 1) < 64

    def write(target, side):
        for y in range(4):
            base = side * 160 + y * ROWS
            for frame in range(4):
                at = (frame // 2) * 384 + (frame % 2) * 128
                odd = frame % 2

                def part(group, offset):
                    row = base + group * 8
                    return block[row : row + 8, at + offset : at + offset + 128]

                def main(group):
                    if odd:
                        return jnp.where(left, part(group, 128), part(group, 0))
                    return part(group, 0)

                def rest(group, place):
                    value = part(group, 128)
                    return value if place == odd else pltpu.roll(value, 64, 1)

                tiles = compact(main, rest)
                for x in range(4):
                    target[y * 4 + x, frame] = jnp.concatenate(
                        tiles[2 * x : 2 * x + 2], axis=0
                    ).astype(BF)

    @pl.when(core == 0)
    def _():
        write(keep, 0)
        write(send, 1)

    @pl.when(core == 1)
    def _():
        write(keep, 1)
        write(send, 0)


def gradients(live, notes, mixed, dshift, moments, gain, patch):
    whole = lambda *dims: pl.BlockSpec(dims, lambda i: (0,) * len(dims))
    halves = pl.BlockSpec((16, 4, 16, COLS), lambda i: (0, i, 0, 0))
    return call(
        grad_body,
        (
            shape((CAP, CH, COLS), BF),
            shape((16, 16, 16, COLS), BF),
            shape((16, 16, 16, COLS), BF),
            shape((CH, COLS)),
            shape((1, CH, COLS), BF),
            shape((1, CH, COLS), BF),
        ),
        [
            SMEM,
            whole(32, 2, 384),
            whole(CAP, CH, COLS),
            whole(CAP, CH, COLS),
            whole(2, CH, COLS),
            whole(CH, COLS),
            pl.BlockSpec(memory_space=pltpu.HBM),
        ],
        [
            pltpu.VMEM((CH, CAP * COLS), BF),
            pltpu.VMEM((4, 768, CAP * COLS), BF),
            pltpu.SemaphoreType.DMA((4,)),
        ],
        grid=(4,),
        out_specs=(
            whole(CAP, CH, COLS),
            halves,
            halves,
            whole(CH, COLS),
            whole(1, CH, COLS),
            whole(1, CH, COLS),
        ),
        cost=7,
        room=24,
    )(live, notes, mixed, dshift, moments, gain, patch)


def add_body(keep, passed, out):
    for index in range(16):
        out[index] = (keep[index].astype(F32) + passed[index].astype(F32)).astype(BF)


def add_pair(keep, passed):
    return call(
        add_body, shape((16, 16, 16, COLS), BF), [VMEM, VMEM], out_specs=VMEM
    )(keep, passed)


def plane_body(parts, riders, out):
    piece = spot("core") * 4 + spot("y")
    ride = jnp.zeros((8, COLS), F32)
    for group in range(5):
        at = pl.multiple_of(piece * ROWS + group * 8, 8)
        ride = ride + pltpu.roll(riders[pl.ds(at, 8), :], 64 + 4 * group, 1)
    ride = jnp.where(spot("x") == 3, ride, 0.0)
    ride = jnp.concatenate([jnp.zeros((8, COLS), F32), ride], axis=0)
    for frame in range(16):
        total = parts[0, frame].astype(F32)
        for part in range(1, 16):
            total = total + parts[part, frame].astype(F32)
        out[frame] = (total + ride).astype(BF)


def plane_sum(parts, riders):
    return call(
        plane_body, shape((16, 16, COLS), BF), [VMEM, VMEM], out_specs=VMEM
    )(parts, riders)


def frame_body(frames, out):
    total = frames[0].astype(F32)
    for frame in range(1, 16):
        total = total + frames[frame].astype(F32)
    lane = lax.broadcasted_iota(jnp.int32, (16, COLS), 1)
    row = lax.broadcasted_iota(jnp.int32, (16, COLS), 0)
    leads = lane % 2 == 0
    both = total + jnp.where(leads, pltpu.roll(total, COLS - 1, 1), pltpu.roll(total, 1, 1))
    high = both.astype(BF).astype(F32)
    riding = (lane >= 64) & (row >= 8) & (spot("x") == 3)
    value = jnp.where(riding, jnp.where(leads, high, both - high), total).astype(BF)
    for tile in range(32):
        out[tile] = value


def frame_sum(frames):
    return call(frame_body, shape((32, 16, COLS), BF), [VMEM], out_specs=VMEM)(frames)


def adam_body(
    tiles, master, first, second, grad, weight_out, first_out, second_out, gain, bias, square
):
    odd = (spot("fsdp") % 2) == 1
    lane = lax.broadcasted_iota(jnp.int32, (8, COLS), 1)
    for core in range(2):
        for y in range(4):
            part = [
                tiles[y * 8 + (index // 2) * 2 + core, (index % 2) * 8 : (index % 2) * 8 + 8, :]
                for index in range(8)
            ]
            part = [value.astype(F32) for value in part]
            for group in range(5):
                at = (core * 4 + y) * ROWS + group * 8
                main = part[group]
                rest = part[5 + group // 2]
                if group % 2:
                    rest = pltpu.roll(rest, 64, 1)
                ride = pltpu.roll(part[7], COLS - 4 * group, 1)
                square[at : at + 8, 0:128] = jnp.where(odd, pltpu.roll(main, 64, 1), main)
                square[at : at + 8, 128:256] = jnp.where(lane < 64, rest, ride)
    square[CH:, :] = jnp.zeros((64, LANES), F32)
    turned = jnp.transpose(square[...])[:, :CH] * SCALE
    gain[...] = (turned[192:193] + turned[193:194])[0]
    bias[...] = (turned[194:195] + turned[195:196])[0]
    value = turned[:SHARD]
    grad[...] = value
    new_first = 0.9 * first[...] + 0.1 * value
    new_second = 0.999 * second[...] + 0.001 * value * value
    first_out[...] = new_first
    second_out[...] = new_second
    first_fix = new_first / (1.0 - 0.9**10)
    second_fix = new_second / (1.0 - 0.999**10)
    weight_out[...] = master[...] - 0.01 * first_fix / (jnp.sqrt(second_fix) + 1e-08)


def adam(tiles, master, first, second):
    return call(
        adam_body,
        (shape((SHARD, CH)),) * 4 + (shape((CH,)),) * 2,
        [VMEM] * 4,
        [pltpu.VMEM((384, LANES), F32)],
        out_specs=(VMEM,) * 6,
    )(tiles, master, first, second)


def back_body(live_ref, weight, pre, above, below, out, field, total):
    live = live_ref[0, 0]

    def put(tap, r, value):
        field[tap, :, r * COLS : (r + 1) * COLS] = value.astype(BF)

    for slot in range(CAP + 2):
        store_taps(framed_row(slot, pre, above, below, live), put, slot, True)
    for tap in range(9):
        start = tap * CH
        parts = []
        while start < (tap + 1) * CH:
            frame = start // SHARD
            stop = min((frame + 1) * SHARD, (tap + 1) * CH)
            parts.append(weight[:, start + 12 * frame : stop + 12 * frame])
            start = stop
        left = jnp.concatenate(parts, axis=1)
        block = lax.dot_general(
            left, field[tap], (((0,), (0,)), ((), ())), preferred_element_type=F32
        )
        total[...] = block if tap == 0 else total[...] + block
    for r in range(CAP):
        value = total[:, r * COLS : (r + 1) * COLS]
        out[r] = jnp.where(r < live, value, 0.0).astype(BF)


def back(live, weight, pre, above, below):
    return call(
        back_body,
        shape((CAP, CH, COLS), BF),
        [SMEM] + [VMEM] * 4,
        [pltpu.VMEM((9, CH, CAP * COLS), BF), pltpu.VMEM((CH, CAP * COLS), F32)],
        out_specs=VMEM,
        cost=14,
        room=24,
    )(live, weight, pre, above, below)


def beside(first_row, last_row):
    count = 32
    ends = count - 1
    above = lax.ppermute(last_row, TILE, [(i, (i + 1) % count) for i in range(ends)])
    below = lax.ppermute(first_row, TILE, [((i + 1) % count, i) for i in range(ends)])
    return above, below


def other_core(value):
    return lax.ppermute(value, "core", [(0, 1), (1, 0)])


def local(
    images, tile_rows, cotangent, master_weight, norm_gain, norm_bias, first_moment, second_moment
):
    own = jnp.swapaxes(images[0, 0], 1, 2)
    upstream = jnp.swapaxes(cotangent[0, 0], 1, 2)
    packed = pack(master_weight)
    along_z = lax.all_to_all(packed, "fsdp", 0, 0)
    above, below = beside(*edges(tile_rows, own, packed))
    patch = patches(tile_rows, own, above, below)
    patch = pltpu.with_memory_space_constraint(patch, pltpu.HBM)
    along_z, patch = lax.optimization_barrier((along_z, patch))
    mine = lax.all_to_all(copies(along_z, 16), ("y", "x"), 0, 0)
    other = other_core(mine)
    mixed, weight, message = forward(tile_rows, mine, other, patch)
    stats = lax.all_to_all(message, TILE, 0, 0)
    gain = jnp.broadcast_to(norm_gain[:, None], (CH, COLS))
    bias = jnp.broadcast_to(norm_bias[:, None], (CH, COLS))
    active, dshift, moments, note = normalize(tile_rows, stats, mixed, upstream, gain, bias)
    notes = lax.all_to_all(note, TILE, 0, 0)
    pre, keep, send, riders, pre_first, pre_last = gradients(
        tile_rows, notes, mixed, dshift, moments, gain, patch
    )
    above_grad, below_grad = beside(pre_first, pre_last)
    parts = lax.all_to_all(add_pair(keep, other_core(send)), ("y", "x"), 0, 0)
    frames = lax.all_to_all(plane_sum(parts, riders), "fsdp", 0, 0)
    image_grad = back(tile_rows, weight, pre, above_grad, below_grad)
    tiles = lax.all_to_all(frame_sum(frames), TILE, 0, 0)
    grad, new_weight, new_first, new_second, gain_grad, bias_grad = adam(
        tiles, master_weight, first_moment, second_moment
    )
    return (
        jnp.swapaxes(active, 1, 2)[None, None],
        jnp.swapaxes(image_grad, 1, 2)[None, None],
        grad,
        new_weight,
        new_first,
        new_second,
        gain_grad,
        bias_grad,
    )


def solution(mesh):
    fine = Mesh(mesh.devices.reshape(4, 4, 2, 16), ("y", "x", "core", "fsdp"))
    pixels = P("fsdp", TILE, None, None, None)
    rows = P("fsdp", None)
    return jax.shard_map(
        local,
        mesh=fine,
        in_specs=(pixels, P("fsdp", TILE), pixels, rows, P(), P(), rows, rows),
        out_specs=(pixels, pixels, rows, rows, rows, rows, P(), P()),
        check_vma=False,
    )
```

```python
import functools
import jax
import jax.numpy as jnp
from jax import lax
from jax.experimental import pallas as pl
from jax.experimental.pallas import tpu as pltpu
from jax.sharding import Mesh, PartitionSpec as P

TILE = ("y", "x", "core")
CH = 320
PER = 10
COLS = 128
CAP = 8
SHARD = 180
WIDE = 192
DEEP = 16 * WIDE
ROWS = 40
LANES = 256
POPULATION = 204800.0
SCALE = 327680.0 ** -0.5
BF = jnp.bfloat16
F32 = jnp.float32
VMEM = pl.BlockSpec(memory_space=pltpu.VMEM)
SMEM = pl.BlockSpec(memory_space=pltpu.SMEM)


def place_of(y, x):
    return y * 4 + (x if y % 2 == 0 else 3 - x)


SNAKE = sorted(range(16), key=lambda i: place_of(i // 4, i % 4))
PLANES = [[2 * i + core for i in SNAKE] for core in range(2)]


def spot(name):
    return lax.axis_index(name)


def call(body, outs, ins, scratch=(), grid=None, cost=1, room=16, **more):
    if grid is not None:
        more["grid"] = grid
    return pl.pallas_call(
        body,
        out_shape=outs,
        in_specs=ins,
        scratch_shapes=list(scratch),
        compiler_params=pltpu.CompilerParams(vmem_limit_bytes=room << 20),
        cost_estimate=pl.CostEstimate(
            flops=cost * 1000000000, bytes_accessed=cost << 21, transcendentals=0
        ),
        **more,
    )


def shape(dims, kind=F32):
    return jax.ShapeDtypeStruct(dims, kind)


def compact(main, rest):
    left = lax.broadcasted_iota(jnp.int32, (8, COLS), 1) < 64
    tiles = [main(group) for group in range(5)]
    for low in (0, 2):
        tiles.append(jnp.where(left, rest(low, 0), rest(low + 1, 1)))
    tiles.append(jnp.where(left, rest(4, 0), 0.0))
    return tiles


def pack_body(weight, out, padded, turned, tight):
    padded[...] = jnp.zeros(padded.shape, F32)
    padded[0:SHARD, 0:CH] = weight[...]
    turned[...] = jnp.transpose(padded[...])
    piece = spot("core") * 4 + spot("y")
    rows = turned[pl.ds(pl.multiple_of(piece * ROWS, 8), ROWS), :]
    odd = (spot("fsdp") % 2) == 1

    def main(group):
        value = rows[group * 8 : group * 8 + 8, 0:128]
        return jnp.where(odd, pltpu.roll(value, 64, 1), value)

    def rest(group, side):
        value = rows[group * 8 : group * 8 + 8, 128:256]
        return pltpu.roll(value, 64, 1) if side else value

    for index, tile in enumerate(compact(main, rest)):
        tight[index * 8 : index * 8 + 8] = tile
    mine = tight[pl.ds(pl.multiple_of(spot("x") * 16, 8), 16), :].astype(BF)
    for frame in range(16):
        out[frame] = mine


def pack(weight):
    return call(
        pack_body,
        shape((16, 16, COLS), BF),
        [VMEM],
        [
            pltpu.VMEM((256, 384), F32),
            pltpu.VMEM((384, 256), F32),
            pltpu.VMEM((64, COLS), F32),
        ],
        out_specs=VMEM,
    )(weight)


def edge_body(live_ref, own, token, first_row, last_row):
    first_row[0] = own[0]
    last_row[0] = own[live_ref[0, 0] - 1]


def edges(live, own, token):
    return call(
        edge_body,
        (shape((1, CH, COLS), BF),) * 2,
        [SMEM, VMEM, pl.BlockSpec(memory_space=pl.ANY)],
        out_specs=(VMEM, VMEM),
    )(live, own, token)


def copies_body(value, out):
    for index in range(out.shape[0]):
        out[index] = value[...]


def copies(value, count):
    return call(
        copies_body, shape((count,) + value.shape, value.dtype), [VMEM], out_specs=VMEM
    )(value)


def store_taps(row, field, slot, negate):
    lane = lax.broadcasted_iota(jnp.int32, (CH, COLS), 1)
    for b in range(3):
        turn = (1 - b) if not negate else (b - 1)
        if turn == 0:
            moved = row
        elif turn == 1:
            moved = jnp.where(lane == 0, 0.0, pltpu.roll(row, 1, 1))
        else:
            moved = jnp.where(lane == COLS - 1, 0.0, pltpu.roll(row, COLS - 1, 1))
        for a in range(3):
            up = a if not negate else 2 - a
            r = slot - up
            if 0 <= r < CAP:
                field(3 * a + b, r, moved)


def framed_row(slot, own, above, below, live):
    if slot == 0:
        return above[0].astype(F32)
    base = own[slot - 1].astype(F32) if slot <= CAP else jnp.zeros((CH, COLS), F32)
    if slot == 1:
        return base
    under = below[0].astype(F32)
    return jnp.where(slot - 1 < live, base, jnp.where(slot - 1 == live, under, 0.0))


def patch_body(live_ref, own, above, below, out, wide):
    live = live_ref[0, 0]

    def put(tap, r, value):
        start = tap * CH
        while start < (tap + 1) * CH:
            frame = start // SHARD
            stop = min((frame + 1) * SHARD, (tap + 1) * CH)
            wide[r, start + 12 * frame : stop + 12 * frame, :] = value[
                start - tap * CH : stop - tap * CH
            ]
            start = stop

    for frame in range(16):
        first = frame * WIDE + SHARD
        wide[:, first : first + 12, :] = jnp.zeros((CAP, 12, COLS), F32)
    for slot in range(CAP + 2):
        store_taps(framed_row(slot, own, above, below, live), put, slot, False)
    for r in range(CAP):
        out[:, r * COLS : (r + 1) * COLS] = wide[r].astype(BF)


def patches(live, own, above, below):
    return call(
        patch_body,
        shape((DEEP, CAP * COLS), BF),
        [SMEM, VMEM, VMEM, VMEM],
        [pltpu.VMEM((CAP, DEEP, COLS), F32)],
        out_specs=VMEM,
        cost=8,
        room=30,
    )(live, own, above, below)


def one_hot():
    channel = lax.broadcasted_iota(jnp.int32, (CH, COLS), 0)
    lane = lax.broadcasted_iota(jnp.int32, (CH, COLS), 1) * PER
    return jnp.where((channel >= lane) & (channel < lane + PER), 1.0, 0.0)


def to_groups(column, hot):
    return jnp.sum(column * hot, axis=0, keepdims=True)


def from_groups(row, hot):
    return jnp.broadcast_to(jnp.sum(row * hot, axis=1, keepdims=True), (CH, COLS))


def forward_body(live_ref, mine, other, patch, mixed, weight, message, held, arrived):
    step = pl.program_id(0)

    def block_copy(index):
        return pltpu.make_async_copy(
            patch.at[:, index * 256 : (index + 1) * 256], held.at[index], arrived.at[index]
        )

    @pl.when(step == 0)
    def _():
        for index in range(4):
            block_copy(index).start()
        left = lax.broadcasted_iota(jnp.int32, (8, COLS), 1) < 64
        for half, source in ((0, mine), (1, other)):
            side = (spot("core") + half) % 2
            for y in range(4):
                base = pl.multiple_of(side * 160 + y * ROWS, 8)
                for pair in range(8):
                    at = pair * 384

                    def tile(frame, index):
                        row = (index % 2) * 8
                        value = source[place_of(y, index // 2), 2 * pair + frame, row : row + 8, :]
                        return value.astype(F32)

                    even = [tile(0, index) for index in range(8)]
                    odd = [tile(1, index) for index in range(8)]
                    first, middle, last = [], [], []
                    for group in range(5):
                        rest = [even[5 + group // 2], odd[5 + group // 2]]
                        turn = 1 - group % 2
                        rest[turn] = pltpu.roll(rest[turn], 64, 1)
                        first.append(even[group])
                        middle.append(jnp.where(left, rest[0], odd[group]))
                        last.append(jnp.where(left, odd[group], rest[1]))
                    for place, parts in ((0, first), (128, middle), (256, last)):
                        weight[pl.ds(base, ROWS), at + place : at + place + 128] = (
                            jnp.concatenate(parts, axis=0).astype(BF)
                        )

    for index in range(4):

        @pl.when(step == index)
        def _():
            block_copy(index).wait()

    block = jnp.dot(weight[...], held[step], preferred_element_type=F32)
    mixed[2 * step] = block[:, :128]
    mixed[2 * step + 1] = block[:, 128:]

    @pl.when(step == 3)
    def _():
        live = live_ref[0, 0]
        hot = one_hot()
        total = jnp.zeros((CH, COLS), F32)
        for r in range(CAP):
            total = total + jnp.where(r < live, mixed[r], 0.0)
        column = jnp.broadcast_to(jnp.sum(total, axis=1, keepdims=True), (CH, COLS))
        sums = to_groups(column, hot)
        count = live.astype(F32) * (COLS * PER)
        mean = from_groups(sums / count, hot)
        square = jnp.zeros((CH, COLS), F32)
        for r in range(CAP):
            away = mixed[r] - mean
            square = square + jnp.where(r < live, away * away, 0.0)
        column = jnp.broadcast_to(jnp.sum(square, axis=1, keepdims=True), (CH, COLS))
        squares = to_groups(column, hot)
        line = lax.broadcasted_iota(jnp.int32, (8, COLS), 0)
        note = jnp.where(line == 0, sums, jnp.where(line == 1, squares, count))
        for tile in range(32):
            message[tile] = note


def forward(live, mine, other, patch):
    whole = lambda *dims: pl.BlockSpec(dims, lambda i: (0,) * len(dims))
    return call(
        forward_body,
        (shape((CAP, CH, COLS)), shape((CH, DEEP), BF), shape((32, 8, COLS))),
        [
            SMEM,
            whole(16, 16, 16, COLS),
            whole(16, 16, 16, COLS),
            pl.BlockSpec(memory_space=pltpu.HBM),
        ],
        [pltpu.VMEM((4, DEEP, 256), BF), pltpu.SemaphoreType.DMA((4,))],
        grid=(4,),
        out_specs=(whole(CAP, CH, COLS), whole(CH, DEEP), whole(32, 8, COLS)),
        cost=6,
        room=24,
    )(live, mine, other, patch)


def to_row(value, spare):
    spare[...] = jnp.zeros(spare.shape, F32)
    spare[0:CH, :] = value
    return jnp.sum(jnp.transpose(spare[...]), axis=0, keepdims=True)


def norm_body(
    live_ref, stats, mixed, upstream, gain, bias, active, dshift, moments, message, sums, spare
):
    live = live_ref[0, 0]
    hot = one_hot()
    part, square, count = stats[:, 0, :], stats[:, 1, :], stats[:, 2, :]
    mean_row = jnp.sum(part, axis=0, keepdims=True) * (1.0 / POPULATION)
    offset = part / count - mean_row
    spread = jnp.sum(square + count * offset * offset, axis=0, keepdims=True)
    inverse_row = lax.rsqrt(spread * (1.0 / POPULATION) + 1e-05)
    moments[0] = from_groups(mean_row, hot)
    moments[1] = from_groups(inverse_row, hot)
    sums[...] = jnp.zeros(sums.shape, F32)

    def row(r, carry):
        alive = r < live
        for part in range(8):
            at = pl.ds(part * ROWS, ROWS)
            normed = (mixed[r, at, :] - moments[0, at, :]) * moments[1, at, :]
            shifted = normed * gain[at, :] + bias[at, :]
            gate = jax.nn.sigmoid(shifted)
            active[r, at, :] = jnp.where(alive, shifted * gate, 0.0).astype(BF)
            above = upstream[r, at, :].astype(F32)
            change = jnp.where(alive, above * gate * (1.0 + shifted * (1.0 - gate)), 0.0)
            dshift[r, at, :] = change
            sums[0, at, :] += change * normed
            sums[1, at, :] += change
        return carry

    lax.fori_loop(0, CAP, row, 0)
    gain_row = to_row(sums[0], spare)
    bias_row = to_row(sums[1], spare)
    line = lax.broadcasted_iota(jnp.int32, (8, 384), 0)
    note = jnp.where(line == 0, gain_row, bias_row)
    for tile in range(32):
        message[tile] = note[0:2]


def normalize(live, stats, mixed, upstream, gain, bias):
    return call(
        norm_body,
        (
            shape((CAP, CH, COLS), BF),
            shape((CAP, CH, COLS)),
            shape((2, CH, COLS)),
            shape((32, 2, 384)),
        ),
        [SMEM] + [VMEM] * 5,
        [pltpu.VMEM((2, CH, COLS), F32), pltpu.VMEM((384, COLS), F32)],
        out_specs=(VMEM,) * 4,
        cost=4,
    )(live, stats, mixed, upstream, gain, bias)


def to_column(row):
    return jnp.transpose(jnp.broadcast_to(row, (COLS, 384)))[:CH]


def grad_body(
    live_ref,
    notes,
    mixed,
    dshift,
    moments,
    gain,
    patch,
    pre,
    keep,
    send,
    riders,
    first_row,
    last_row,
    field,
    held,
    arrived,
):
    step = pl.program_id(0)
    core = spot("core")

    def block_copy(index):
        return pltpu.make_async_copy(
            patch.at[index * 768 : (index + 1) * 768], held.at[index], arrived.at[index]
        )

    @pl.when(step == 0)
    def _():
        for index in range(4):
            block_copy(index).start()
        live = live_ref[0, 0]
        hot = one_hot()
        totals = jnp.sum(notes[...], axis=0)
        gain_total = to_column(totals[0:1])
        bias_total = to_column(totals[1:2])
        lane = lax.broadcasted_iota(jnp.int32, (CH, COLS), 1)
        gain_high = gain_total.astype(BF).astype(F32)
        bias_high = bias_total.astype(BF).astype(F32)
        packed = jnp.where(lane == 0, gain_high, jnp.where(lane == 1, gain_total - gain_high, 0.0))
        packed = jnp.where(lane == 2, bias_high, packed)
        riders[...] = jnp.where(lane == 3, bias_total - bias_high, packed)
        share = 1.0 / POPULATION
        delta = from_groups(to_groups(bias_total * gain[...], hot) * share, hot)
        cross = from_groups(to_groups(gain_total * gain[...], hot) * share, hot)
        for r in range(CAP):
            normed = (mixed[r] - moments[0]) * moments[1]
            value = moments[1] * (dshift[r] * gain[...] - delta - normed * cross)
            value = jnp.where(r < live, value, 0.0).astype(BF)
            pre[r] = value
            field[:, r * COLS : (r + 1) * COLS] = value
        first_row[0] = pre[0]
        last_row[0] = pre[live - 1]

    for index in range(4):

        @pl.when(step == index)
        def _():
            block_copy(index).wait()

    block = lax.dot_general(
        field[...], held[step], (((1,), (1,)), ((), ())), preferred_element_type=F32
    )

    left = lax.broadcasted_iota(jnp.int32, (8, COLS), 1) < 64

    def write(target, side):
        for y in range(4):
            base = side * 160 + y * ROWS
            for frame in range(4):
                at = (frame // 2) * 384 + (frame % 2) * 128
                odd = frame % 2

                def part(group, offset):
                    row = base + group * 8
                    return block[row : row + 8, at + offset : at + offset + 128]

                def main(group):
                    if odd:
                        return jnp.where(left, part(group, 128), part(group, 0))
                    return part(group, 0)

                def rest(group, place):
                    value = part(group, 128)
                    return value if place == odd else pltpu.roll(value, 64, 1)

                tiles = compact(main, rest)
                for x in range(4):
                    target[place_of(y, x), frame] = jnp.concatenate(
                        tiles[2 * x : 2 * x + 2], axis=0
                    ).astype(BF)

    @pl.when(core == 0)
    def _():
        write(keep, 0)
        write(send, 1)

    @pl.when(core == 1)
    def _():
        write(keep, 1)
        write(send, 0)


def gradients(live, notes, mixed, dshift, moments, gain, patch):
    whole = lambda *dims: pl.BlockSpec(dims, lambda i: (0,) * len(dims))
    halves = pl.BlockSpec((16, 4, 16, COLS), lambda i: (0, i, 0, 0))
    return call(
        grad_body,
        (
            shape((CAP, CH, COLS), BF),
            shape((16, 16, 16, COLS), BF),
            shape((16, 16, 16, COLS), BF),
            shape((CH, COLS)),
            shape((1, CH, COLS), BF),
            shape((1, CH, COLS), BF),
        ),
        [
            SMEM,
            whole(32, 2, 384),
            whole(CAP, CH, COLS),
            whole(CAP, CH, COLS),
            whole(2, CH, COLS),
            whole(CH, COLS),
            pl.BlockSpec(memory_space=pltpu.HBM),
        ],
        [
            pltpu.VMEM((CH, CAP * COLS), BF),
            pltpu.VMEM((4, 768, CAP * COLS), BF),
            pltpu.SemaphoreType.DMA((4,)),
        ],
        grid=(4,),
        out_specs=(
            whole(CAP, CH, COLS),
            halves,
            halves,
            whole(CH, COLS),
            whole(1, CH, COLS),
            whole(1, CH, COLS),
        ),
        cost=7,
        room=24,
    )(live, notes, mixed, dshift, moments, gain, patch)


def add_body(keep, passed, out):
    for index in range(16):
        out[index] = (keep[index].astype(F32) + passed[index].astype(F32)).astype(BF)


def add_pair(keep, passed):
    return call(
        add_body, shape((16, 16, 16, COLS), BF), [VMEM, VMEM], out_specs=VMEM
    )(keep, passed)


def plane_body(parts, riders, out):
    piece = spot("core") * 4 + spot("y")
    ride = jnp.zeros((8, COLS), F32)
    for group in range(5):
        at = pl.multiple_of(piece * ROWS + group * 8, 8)
        ride = ride + pltpu.roll(riders[pl.ds(at, 8), :], 64 + 4 * group, 1)
    ride = jnp.where(spot("x") == 3, ride, 0.0)
    ride = jnp.concatenate([jnp.zeros((8, COLS), F32), ride], axis=0)
    for frame in range(16):
        total = parts[0, frame].astype(F32)
        for part in range(1, 16):
            total = total + parts[part, frame].astype(F32)
        out[frame] = (total + ride).astype(BF)


def plane_sum(parts, riders):
    return call(
        plane_body, shape((16, 16, COLS), BF), [VMEM, VMEM], out_specs=VMEM
    )(parts, riders)


def frame_body(frames, out):
    total = frames[0].astype(F32)
    for frame in range(1, 16):
        total = total + frames[frame].astype(F32)
    lane = lax.broadcasted_iota(jnp.int32, (16, COLS), 1)
    row = lax.broadcasted_iota(jnp.int32, (16, COLS), 0)
    leads = lane % 2 == 0
    both = total + jnp.where(leads, pltpu.roll(total, COLS - 1, 1), pltpu.roll(total, 1, 1))
    high = both.astype(BF).astype(F32)
    riding = (lane >= 64) & (row >= 8) & (spot("x") == 3)
    value = jnp.where(riding, jnp.where(leads, high, both - high), total).astype(BF)
    for tile in range(32):
        out[tile] = value


def frame_sum(frames):
    return call(frame_body, shape((32, 16, COLS), BF), [VMEM], out_specs=VMEM)(frames)


def adam_body(
    tiles, master, first, second, grad, weight_out, first_out, second_out, gain, bias, square
):
    odd = (spot("fsdp") % 2) == 1
    lane = lax.broadcasted_iota(jnp.int32, (8, COLS), 1)
    for core in range(2):
        for y in range(4):
            part = [
                tiles[y * 8 + (index // 2) * 2 + core, (index % 2) * 8 : (index % 2) * 8 + 8, :]
                for index in range(8)
            ]
            part = [value.astype(F32) for value in part]
            for group in range(5):
                at = (core * 4 + y) * ROWS + group * 8
                main = part[group]
                rest = part[5 + group // 2]
                if group % 2:
                    rest = pltpu.roll(rest, 64, 1)
                ride = pltpu.roll(part[7], COLS - 4 * group, 1)
                square[at : at + 8, 0:128] = jnp.where(odd, pltpu.roll(main, 64, 1), main)
                square[at : at + 8, 128:256] = jnp.where(lane < 64, rest, ride)
    square[CH:, :] = jnp.zeros((64, LANES), F32)
    turned = jnp.transpose(square[...])[:, :CH] * SCALE
    gain[...] = (turned[192:193] + turned[193:194])[0]
    bias[...] = (turned[194:195] + turned[195:196])[0]
    value = turned[:SHARD]
    grad[...] = value
    new_first = 0.9 * first[...] + 0.1 * value
    new_second = 0.999 * second[...] + 0.001 * value * value
    first_out[...] = new_first
    second_out[...] = new_second
    first_fix = new_first / (1.0 - 0.9**10)
    second_fix = new_second / (1.0 - 0.999**10)
    weight_out[...] = master[...] - 0.01 * first_fix / (jnp.sqrt(second_fix) + 1e-08)


def adam(tiles, master, first, second):
    return call(
        adam_body,
        (shape((SHARD, CH)),) * 4 + (shape((CH,)),) * 2,
        [VMEM] * 4,
        [pltpu.VMEM((384, LANES), F32)],
        out_specs=(VMEM,) * 6,
    )(tiles, master, first, second)


def back_body(live_ref, weight, pre, above, below, out, field, total):
    live = live_ref[0, 0]

    def put(tap, r, value):
        field[tap, :, r * COLS : (r + 1) * COLS] = value.astype(BF)

    for slot in range(CAP + 2):
        store_taps(framed_row(slot, pre, above, below, live), put, slot, True)
    for tap in range(9):
        start = tap * CH
        parts = []
        while start < (tap + 1) * CH:
            frame = start // SHARD
            stop = min((frame + 1) * SHARD, (tap + 1) * CH)
            parts.append(weight[:, start + 12 * frame : stop + 12 * frame])
            start = stop
        left = jnp.concatenate(parts, axis=1)
        block = lax.dot_general(
            left, field[tap], (((0,), (0,)), ((), ())), preferred_element_type=F32
        )
        total[...] = block if tap == 0 else total[...] + block
    for r in range(CAP):
        value = total[:, r * COLS : (r + 1) * COLS]
        out[r] = jnp.where(r < live, value, 0.0).astype(BF)


def back(live, weight, pre, above, below):
    return call(
        back_body,
        shape((CAP, CH, COLS), BF),
        [SMEM] + [VMEM] * 4,
        [pltpu.VMEM((9, CH, CAP * COLS), BF), pltpu.VMEM((CH, CAP * COLS), F32)],
        out_specs=VMEM,
        cost=14,
        room=24,
    )(live, weight, pre, above, below)


def beside(first_row, last_row):
    count = 32
    ends = count - 1
    above = lax.ppermute(last_row, TILE, [(i, (i + 1) % count) for i in range(ends)])
    below = lax.ppermute(first_row, TILE, [((i + 1) % count, i) for i in range(ends)])
    return above, below


def other_core(value):
    return lax.ppermute(value, "core", [(0, 1), (1, 0)])


def local(
    images, tile_rows, cotangent, master_weight, norm_gain, norm_bias, first_moment, second_moment
):
    own = jnp.swapaxes(images[0, 0], 1, 2)
    upstream = jnp.swapaxes(cotangent[0, 0], 1, 2)
    packed = pack(master_weight)
    along_z = lax.all_to_all(packed, "fsdp", 0, 0)
    above, below = beside(*edges(tile_rows, own, packed))
    patch = patches(tile_rows, own, above, below)
    patch = pltpu.with_memory_space_constraint(patch, pltpu.HBM)
    along_z, patch = lax.optimization_barrier((along_z, patch))
    mine = lax.all_to_all(copies(along_z, 16), TILE, 0, 0, axis_index_groups=PLANES)
    other = other_core(mine)
    mixed, weight, message = forward(tile_rows, mine, other, patch)
    stats = lax.all_to_all(message, TILE, 0, 0)
    gain = jnp.broadcast_to(norm_gain[:, None], (CH, COLS))
    bias = jnp.broadcast_to(norm_bias[:, None], (CH, COLS))
    active, dshift, moments, note = normalize(tile_rows, stats, mixed, upstream, gain, bias)
    notes = lax.all_to_all(note, TILE, 0, 0)
    pre, keep, send, riders, pre_first, pre_last = gradients(
        tile_rows, notes, mixed, dshift, moments, gain, patch
    )
    above_grad, below_grad = beside(pre_first, pre_last)
    parts = lax.all_to_all(add_pair(keep, other_core(send)), TILE, 0, 0, axis_index_groups=PLANES)
    frames = lax.all_to_all(plane_sum(parts, riders), "fsdp", 0, 0)
    image_grad = back(tile_rows, weight, pre, above_grad, below_grad)
    tiles = lax.all_to_all(frame_sum(frames), TILE, 0, 0)
    grad, new_weight, new_first, new_second, gain_grad, bias_grad = adam(
        tiles, master_weight, first_moment, second_moment
    )
    return (
        jnp.swapaxes(active, 1, 2)[None, None],
        jnp.swapaxes(image_grad, 1, 2)[None, None],
        grad,
        new_weight,
        new_first,
        new_second,
        gain_grad,
        bias_grad,
    )


def solution(mesh):
    fine = Mesh(mesh.devices.reshape(4, 4, 2, 16), ("y", "x", "core", "fsdp"))
    pixels = P("fsdp", TILE, None, None, None)
    rows = P("fsdp", None)
    return jax.shard_map(
        local,
        mesh=fine,
        in_specs=(pixels, P("fsdp", TILE), pixels, rows, P(), P(), rows, rows),
        out_specs=(pixels, pixels, rows, rows, rows, rows, P(), P()),
        check_vma=False,
    )
```
